256 devices in a mesh: group: 8 (over z), within: 32 (over y, x, core).
Axes of the slice: x: 4, y: 4, z: 8, core: 2. Of those that a mesh axis runs over, the one named last changes fastest.
Arguments:
- vectors: bfloat16 [131072, 768], P(('group', 'within')), may hold values from -6 to 6
- centroids: float32 [16384, 768], P(('group', 'within')), may hold values from -6 to 6
- list_ids: int32 [131072], P(('group', 'within')), may hold values from 0 to 16383, as said below
- codes: int32 [131072, 96], P(('group', 'within')), may hold values from 0 to 255, as said below
- rotation: float32 [768, 768], replicated, may hold values from -0.21875 to 0.21875
Outputs:
- rotated_out: bfloat16 [131072, 768], P(('group', 'within'))
- codebooks: float32 [96, 2048], P('within')
The draws below stay inside these ranges and needn't reach their ends.
Inputs may be any that keep to these rules, and one draw needn't show every extreme that they name: `list_ids`: the rows of the d-th block of 512 rows name only lists d * 64 to (d + 1) * 64 - 1, each of them at least once. `codes`: in subspace m, the rows of the d-th block of 512 rows name codeword 256/2 + (d + m) mod (128) in 2 to 5 consecutive rows (counted round the block) and codewords below 128 elsewhere.
All inputs are finite; a program needn't handle non-finite values.
Results may differ from the reference program's by a relative error of at most 0.012.
Values may be sent and summed in bfloat16 or wider, within the bound.
A program may use at most 64 MiB of HBM per device.

```python
import jax
import jax.numpy as jnp
from jax import lax

D = 768
M = 96
K = 256
DSUB = 8
ROWS_DEV = 512
LISTS_DEV = 64
ALTS = 2
NS_STEPS = 2
ROWS = 131072
LISTS = 16384


def draw_list_ids(key, part):
    blocks = ROWS // ROWS_DEV
    key_perm, key_rand = jax.random.split(key)
    perm_keys = jax.random.split(key_perm, blocks)
    heads = jax.vmap(lambda single: jax.random.permutation(single, LISTS_DEV))(perm_keys).astype(jnp.int32)
    chosen = jax.random.randint(key_rand, (blocks, ROWS_DEV), 0, LISTS_DEV, dtype=jnp.int32)
    chosen = chosen.at[:, :LISTS_DEV].set(heads)
    global_ids = chosen + jnp.arange(blocks, dtype=jnp.int32)[:, None] * LISTS_DEV
    return global_ids.reshape(ROWS).astype(jnp.int32)


def draw_codes(key, part):
    blocks = ROWS // ROWS_DEV
    half = K // 2
    keys = jax.random.split(key, 5)
    first = jax.random.randint(keys[0], (ROWS, M), 0, half, dtype=jnp.int32)
    second = jax.random.randint(keys[1], (ROWS, M), 0, half, dtype=jnp.int32)
    order = jax.random.permutation(keys[2], half).astype(jnp.int32)
    common = jnp.take(order, jnp.minimum(first, second)).reshape(blocks, ROWS_DEV, M)
    block_index = jnp.arange(blocks, dtype=jnp.int32)[:, None]
    subspace = jnp.arange(M, dtype=jnp.int32)[None, :]
    owned = half + (block_index + subspace) % half
    many = jax.random.randint(keys[3], (blocks, M), 2, 6, dtype=jnp.int32)
    start = jax.random.randint(keys[4], (blocks, M), 0, ROWS_DEV, dtype=jnp.int32)
    row_index = jnp.arange(ROWS_DEV, dtype=jnp.int32)[None, :, None]
    position = (row_index - start[:, None, :]) % ROWS_DEV
    chosen = jnp.where(position < many[:, None, :], owned[:, None, :], common)
    return chosen.reshape(ROWS, M).astype(jnp.int32)


def level_of(rng, dims, shards, smallest, top_value):
    def one(axis_at, shards_of):
        steps = jax.random.uniform(jax.random.fold_in(jax.random.fold_in(rng, 6), axis_at), (shards_of,), jnp.float32, smallest / len(shards), top_value / len(shards))
        return jnp.repeat(jnp.exp(steps), dims[axis_at] // shards_of).reshape((-1,) + (1,) * (len(dims) - axis_at - 1))

    factor_of = one(*shards[0])
    for cut in shards[1:]:
        factor_of = factor_of * one(*cut)
    return factor_of


def scatter_about(rng, shape, spread, most, cuts=(), kind=jnp.bfloat16):
    array = jax.random.normal(rng, shape, jnp.float32) * spread
    if len(cuts) > 0:
        array = level_of(rng, shape, cuts, -0.22, 0.18) * array
    return jnp.clip(array, min=-most, max=most).astype(kind)


def setup_inputs(seed: int = 0) -> dict:
    splits = jax.random.split(jax.random.key(seed), 6)
    return {
        "vectors": scatter_about(splits[0], (ROWS, D), 1.0, 6.0, ((0, 256),)),
        "centroids": scatter_about(splits[1], (LISTS, D), 1.0, 6.0, ((0, 256),), jnp.float32),
        "list_ids": draw_list_ids(jax.random.fold_in(splits[5], 71), 0),
        "codes": draw_codes(jax.random.fold_in(splits[5], 71), 0),
        "rotation": scatter_about(splits[4], (D, D), D ** -0.5, 0.21875, (), jnp.float32),
    }


exact_mode = lax.Precision.HIGHEST
epsilon = 1e-06

def polar_factor(cross):
    gram_matrix = jnp.einsum('ik,jk->ij', cross, cross, precision=exact_mode)
    norm_square = jnp.sqrt(jnp.sum(gram_matrix * gram_matrix) + epsilon)
    norm_scale = jnp.sqrt(norm_square)
    current = cross / norm_scale
    gram_matrix = gram_matrix / norm_square
    for iteration in range(NS_STEPS):
        if iteration > 0:
            gram_matrix = jnp.einsum('ik,jk->ij', current, current, precision=exact_mode)
        current = 1.5 * current - 0.5 * jnp.dot(gram_matrix, current, precision=exact_mode)
    return current

def reference(vectors, centroids, list_ids, codes, rotation):
    residual = (vectors.astype(jnp.float32) - jnp.take(centroids, list_ids, axis=0)).astype(jnp.bfloat16)
    segment_ids = (codes + jnp.arange(M, dtype=jnp.int32)[None, :] * K).reshape(-1)
    counts = jax.ops.segment_sum(jnp.ones((ROWS * M,), jnp.float32), segment_ids, num_segments=M * K).reshape(M, K)
    current = rotation
    codebook = jnp.zeros((M, K, DSUB), jnp.float32)
    for alternation in range(ALTS):
        rotated = jnp.dot(residual, current.astype(jnp.bfloat16), preferred_element_type=jnp.float32).astype(jnp.bfloat16)
        values = rotated.astype(jnp.float32).reshape(ROWS * M, DSUB)
        sums = jax.ops.segment_sum(values, segment_ids, num_segments=M * K).reshape(M, K, DSUB)
        codebook = sums / (counts[:, :, None] + 1.0)
        book_table = codebook.astype(jnp.bfloat16).reshape(M * K, DSUB)
        recon = jnp.take(book_table, segment_ids, axis=0).reshape(ROWS, D)
        cross = jnp.dot(residual.T, recon, preferred_element_type=jnp.float32) / ROWS
        current = polar_factor(cross)
    rotated_out = jnp.dot(residual, current.astype(jnp.bfloat16), preferred_element_type=jnp.float32).astype(jnp.bfloat16)
    return (rotated_out, codebook.reshape(M, K * DSUB))
```

```python
import functools

import jax
import jax.numpy as jnp
from jax import lax
from jax.experimental import pallas as pl
from jax.experimental.pallas import tpu as pltpu
from jax.sharding import PartitionSpec as P

K = 256
HALF = K // 2
NS_STEPS = 2
EPSILON = 1e-06
MESH_ID = pl.DeviceIdType.MESH
NT = (((1,), (1,)), ((), ()))
VMEM_LIMIT = 56 * 1024 * 1024


def dot_nt(left, right):
    return lax.dot_general(left, right, NT, preferred_element_type=jnp.float32)


def vmem_spec():
    return pl.BlockSpec(memory_space=pltpu.VMEM)


def local_sums(first, rt, resid_ref, codes_ref, msg_ref, urow_ref, rot_ref, masked_ref):
    width = resid_ref.shape[1]
    rows = resid_ref.shape[0]
    subspaces = codes_ref.shape[0]
    owners = msg_ref.shape[0]
    per_owner = subspaces // owners
    rot_ref[...] = dot_nt(rt, resid_ref[...]).astype(jnp.bfloat16)
    levels = lax.broadcasted_iota(jnp.int32, (HALF, rows), 0)
    device = lax.axis_index("group") * owners + lax.axis_index("within")
    lane = lax.broadcasted_iota(jnp.int32, (8, HALF), 1)
    top = lax.broadcasted_iota(jnp.int32, (16, rows), 0) < 8
    ones_rows = jnp.ones((8, rows), jnp.bfloat16)
    ones_tall = jnp.ones((rows, HALF), jnp.bfloat16)
    ones16 = jnp.ones((16, rows), jnp.bfloat16)

    def step(at, carry):
        base = pl.multiple_of(at * (2 * per_owner), 2 * per_owner)
        for pair in range(per_owner):
            m0 = 2 * pair
            row0 = pl.multiple_of((base + m0) * 8, 16)
            code0 = codes_ref[pl.ds(base + m0, 1), :]
            code1 = codes_ref[pl.ds(base + m0 + 1, 1), :]
            hot0 = (levels == code0).astype(jnp.float32).astype(jnp.bfloat16)
            hot1 = (levels == code1).astype(jnp.float32).astype(jnp.bfloat16)
            hots = jnp.concatenate([hot0, hot1], axis=0)
            left = rot_ref[pl.ds(row0, 16), :]
            both = jnp.where(top, code0, code1)
            upper = jnp.where(both >= HALF, left.astype(jnp.float32), 0.0).astype(jnp.bfloat16)
            masked_ref[pl.ds(row0, 16), :] = upper
            ucol = jnp.dot(upper, ones_tall, preferred_element_type=jnp.float32)
            if first:
                high = jnp.where(both >= HALF, 1.0, 0.0).astype(jnp.bfloat16)
                chigh = jnp.dot(high, ones_tall, preferred_element_type=jnp.float32)
                out = dot_nt(jnp.concatenate([left, ones16], axis=0), hots)
            else:
                out = dot_nt(left, hots)
            for sub in range(2):
                local = m0 + sub
                owner = 2 * at + local // per_owner
                at_owner = local % per_owner
                msg_ref[owner, pl.ds(8 * at_owner, 8), :] = out[
                    8 * sub : 8 * sub + 8, HALF * sub : HALF * sub + HALF
                ]
                place = lane == lax.rem(device + base + local, HALF)
                part = slice(8 * sub, 8 * sub + 8)
                if first:
                    msg_ref[owner, pl.ds(8 * per_owner + at_owner, 1), :] = out[
                        16:17, HALF * sub : HALF * sub + HALF
                    ]
                    dense = jnp.where(place, chigh[part], 0.0)
                    msg_ref[owner, pl.ds(9 * per_owner + at_owner, 1), :] = dense[0:1]
                else:
                    dense = jnp.where(place, ucol[part], 0.0)
                    msg_ref[owner, pl.ds(8 * (per_owner + at_owner), 8), :] = dense
        return carry

    if first:
        msg_ref[...] = jnp.zeros_like(msg_ref)
    lax.fori_loop(0, owners // 2, step, 0)
    urow_ref[:, 0:width] = dot_nt(ones_rows, masked_ref[...])
    high_all = jnp.where(codes_ref[...] >= HALF, 1.0, 0.0)
    high_all = jnp.concatenate(
        [high_all, jnp.zeros((HALF - subspaces, rows), jnp.float32)], axis=0
    ).astype(jnp.bfloat16)
    urow_ref[:, width : width + HALF] = dot_nt(ones_rows, high_all)


def first_kernel(rt_ref, resid_ref, codes_ref, msg_ref, urow_ref, rot_ref, masked_ref):
    local_sums(True, rt_ref[...], resid_ref, codes_ref, msg_ref, urow_ref, rot_ref, masked_ref)


def polar(cross_ref, total_rows):
    chips = cross_ref.shape[1]
    high = cross_ref.shape[2]
    halves = []
    for side in range(2):
        blocks = [cross_ref[side, chip] for chip in range(chips)]
        halves.append(jnp.concatenate(blocks, axis=0))
    cross = jnp.concatenate(halves, axis=1)
    inv_rows = 1.0 / total_rows
    gram = dot_nt(cross, cross) * (inv_rows * inv_rows)
    norm_square = jnp.sqrt(jnp.sum(gram * gram) + EPSILON)
    inv_square = 1.0 / norm_square
    inv_scale = jnp.sqrt(inv_square)
    current = cross.astype(jnp.float32) * (inv_rows * inv_scale)
    gram = gram * inv_square
    for iteration in range(NS_STEPS):
        low = current.astype(jnp.bfloat16)
        if iteration > 0:
            gram = dot_nt(low, low)
        current = 1.5 * current - 0.5 * jnp.dot(
            gram.astype(jnp.bfloat16), low, preferred_element_type=jnp.float32
        )
    return current.astype(jnp.bfloat16)


def next_kernel(total_rows, cross_ref, resid_ref, codes_ref, msg_ref, urow_ref, rot_ref, masked_ref):
    rt = polar(cross_ref, total_rows)
    local_sums(False, rt, resid_ref, codes_ref, msg_ref, urow_ref, rot_ref, masked_ref)


def last_kernel(total_rows, cross_ref, resid_ref, out_ref):
    rt = polar(cross_ref, total_rows)
    out_ref[...] = dot_nt(resid_ref[...], rt).astype(jnp.bfloat16)


def recon_kernel(book_ref, urow_ref, other_ref, codes_ref, resid_ref, cross_ref, rec_ref, ucol_ref):
    owners = book_ref.shape[0]
    subspaces, rows = codes_ref.shape
    width = resid_ref.shape[1]
    per_owner = subspaces // owners
    both = urow_ref[...] + other_ref[...]
    ucol_ref[...] = both[:, 0:width].T
    ccol = both[:, width : width + HALF].T
    top = lax.broadcasted_iota(jnp.int32, (16, HALF), 0) < 8
    for at in range(owners // 2):
        table = jnp.concatenate([book_ref[2 * at], book_ref[2 * at + 1]], axis=0)
        for pair in range(per_owner):
            pieces = []
            for sub in range(2):
                m = at * 2 * per_owner + 2 * pair + sub
                local = 2 * pair + sub
                words = table[8 * local : 8 * local + 8, :].astype(jnp.float32)
                column = ucol_ref[8 * m : 8 * m + 8, 0:1] / (ccol[m : m + 1, 0:1] + 1.0)
                column = jnp.broadcast_to(column, (8, HALF))
                row_pieces = []
                for part in range(rows // HALF):
                    code = jnp.broadcast_to(
                        codes_ref[m : m + 1, HALF * part : HALF * part + HALF], (8, HALF)
                    )
                    low = jnp.take_along_axis(
                        words, jnp.bitwise_and(code, HALF - 1), axis=1, mode="promise_in_bounds"
                    )
                    row_pieces.append(jnp.where(code >= HALF, column, low))
                pieces.append(jnp.concatenate(row_pieces, axis=1))
            first_row = at * 16 * per_owner + 16 * pair
            rec_ref[first_row : first_row + 16, :] = jnp.concatenate(pieces, axis=0).astype(
                jnp.bfloat16
            )
    cross_ref[...] = jnp.dot(rec_ref[...], resid_ref[...], preferred_element_type=jnp.float32)


def greet(within, group, me_w, me_g):
    barrier = pltpu.get_barrier_semaphore()

    def to_within(i, carry):
        pl.semaphore_signal(
            barrier, inc=1, device_id=(me_g, lax.rem(me_w + i, within)), device_id_type=MESH_ID
        )
        return carry

    def to_group(i, carry):
        pl.semaphore_signal(
            barrier, inc=1, device_id=(lax.rem(me_g + i, group), me_w), device_id_type=MESH_ID
        )
        return carry

    lax.fori_loop(1, within, to_within, 0)
    lax.fori_loop(1, group, to_group, 0)
    pl.semaphore_wait(barrier, within + group - 2)


def sums_kernel(
    within, group, last, *refs
):
    if last:
        msg_ref, urow_ref, cnt_ref, book_ref, other_ref, low_ref, up_ref = refs[:7]
        refs = refs[7:]
    else:
        msg_ref, urow_ref, book_ref, other_ref, cnt_ref = refs[:5]
        refs = refs[5:]
    recv1, recv2, s0, r0, s1, r1, s2, r2, s3, r3 = refs
    me_g = lax.axis_index("group")
    me_w = lax.axis_index("within")
    rows = msg_ref.shape[1]
    high = book_ref.shape[1]
    per_owner = high // 8
    greet(within, group, me_w, me_g)

    def send1(i):
        dst = lax.rem(me_w + i, within)
        return pltpu.make_async_remote_copy(
            src_ref=msg_ref.at[dst],
            dst_ref=recv1.at[i - 1],
            send_sem=s1.at[i - 1],
            recv_sem=r1.at[i - 1],
            device_id=(me_g, dst),
            device_id_type=MESH_ID,
        )

    def go1(i, carry):
        send1(i).start()
        return carry

    lax.fori_loop(1, within, go1, 0)
    swap = pltpu.make_async_remote_copy(
        src_ref=urow_ref,
        dst_ref=other_ref,
        send_sem=s0,
        recv_sem=r0,
        device_id=(lax.rem(me_g + group // 2, group), me_w),
        device_id_type=MESH_ID,
    )
    swap.start()

    def take1(i, acc):
        send1(i).wait_recv()
        return acc + recv1[i - 1]

    acc = lax.fori_loop(1, within, take1, msg_ref[me_w])
    recv2[me_g] = acc

    def send2(i, slot):
        dst = lax.rem(me_g + i, group)
        return pltpu.make_async_remote_copy(
            src_ref=recv2.at[slot],
            dst_ref=recv2.at[slot],
            send_sem=s2.at[i - 1],
            recv_sem=r2.at[i - 1],
            device_id=(dst, me_w),
            device_id_type=MESH_ID,
        )

    for i in range(1, group):
        send2(i, me_g).start()
    for i in range(1, group):
        send2(i, lax.rem(me_g + group - i, group)).wait_recv()
    total = recv2[0]
    for i in range(1, group):
        total = total + recv2[i]
    if last:
        counts = cnt_ref[...]
    else:
        counts = total[high : high + 8]
        cnt_ref[...] = counts
    books = []
    for i in range(per_owner):
        books.append(total[8 * i : 8 * i + 8] / (counts[i : i + 1] + 1.0))
    low = jnp.concatenate(books, axis=0)
    book_ref[me_w] = low.astype(jnp.bfloat16)

    def send3(i):
        dst = lax.rem(me_w + i, within)
        return pltpu.make_async_remote_copy(
            src_ref=book_ref.at[me_w],
            dst_ref=book_ref.at[me_w],
            send_sem=s3.at[i - 1],
            recv_sem=r3.at[i - 1],
            device_id=(me_g, dst),
            device_id_type=MESH_ID,
        )

    def go3(i, carry):
        send3(i).start()
        return carry

    lax.fori_loop(1, within, go3, 0)
    if last:
        low_ref[...] = low
        ups = []
        for i in range(per_owner):
            ups.append(
                total[high + 8 * i : high + 8 * i + 8]
                / (counts[per_owner + i : per_owner + i + 1] + 1.0)
            )
        up_ref[...] = jnp.concatenate(ups, axis=0)

    def wait3(i, carry):
        src = lax.rem(me_w + within - i, within)
        pltpu.make_async_remote_copy(
            src_ref=book_ref.at[src],
            dst_ref=book_ref.at[src],
            send_sem=s3.at[i - 1],
            recv_sem=r3.at[i - 1],
            device_id=(me_g, src),
            device_id_type=MESH_ID,
        ).wait_recv()
        send1(i).wait_send()
        send3(i).wait_send()
        return carry

    lax.fori_loop(1, within, wait3, 0)
    for i in range(1, group):
        send2(i, me_g).wait_send()
    swap.wait()


def cross_kernel(within, group, cross_ref, out_ref, *refs):
    st0, rc0, rc1, rc2, s0, r0, s1, r1, s2, r2, s3, r3, s4, r4 = refs
    me_g = lax.axis_index("group")
    me_w = lax.axis_index("within")
    core = lax.rem(me_w, 2)
    chip = me_w // 2
    chips = within // 2
    mate = me_w + 1 - 2 * core
    high, wide = out_ref.shape[2], out_ref.shape[3]

    barrier = pltpu.get_barrier_semaphore()
    pl.semaphore_signal(barrier, inc=1, device_id=(me_g, mate), device_id_type=MESH_ID)

    def to_within(i, carry):
        dst = 2 * lax.rem(chip + i, chips) + core
        pl.semaphore_signal(barrier, inc=1, device_id=(me_g, dst), device_id_type=MESH_ID)
        return carry

    def to_group(i, carry):
        pl.semaphore_signal(
            barrier, inc=1, device_id=(lax.rem(me_g + i, group), me_w), device_id_type=MESH_ID
        )
        return carry

    lax.fori_loop(1, chips, to_within, 0)
    lax.fori_loop(1, group, to_group, 0)
    pl.semaphore_wait(barrier, chips + group - 1)

    mate_at = pl.multiple_of((1 - core) * wide, wide)
    mine_at = pl.multiple_of(core * wide, wide)
    for at in range(chips):
        st0[at] = cross_ref[at * high : at * high + high, pl.ds(mate_at, wide)].astype(
            jnp.bfloat16
        )
    give = pltpu.make_async_remote_copy(
        src_ref=st0, dst_ref=rc0, send_sem=s0, recv_sem=r0,
        device_id=(me_g, mate), device_id_type=MESH_ID,
    )
    give.start()
    give.wait()

    for at in range(chips):
        st0[at] = (
            cross_ref[at * high : at * high + high, pl.ds(mine_at, wide)]
            + rc0[at].astype(jnp.float32)
        ).astype(jnp.bfloat16)

    def send1(i):
        dst = lax.rem(chip + i, chips)
        return pltpu.make_async_remote_copy(
            src_ref=st0.at[dst], dst_ref=rc1.at[i - 1],
            send_sem=s1.at[i - 1], recv_sem=r1.at[i - 1],
            device_id=(me_g, 2 * dst + core), device_id_type=MESH_ID,
        )

    def go1(i, carry):
        send1(i).start()
        return carry

    lax.fori_loop(1, chips, go1, 0)

    def take1(i, acc):
        send1(i).wait_recv()
        return acc + rc1[i - 1].astype(jnp.float32)

    acc = lax.fori_loop(1, chips, take1, st0[chip].astype(jnp.float32))
    rc2[me_g] = acc.astype(jnp.bfloat16)

    def send2(i, slot):
        dst = lax.rem(me_g + i, group)
        return pltpu.make_async_remote_copy(
            src_ref=rc2.at[slot], dst_ref=rc2.at[slot],
            send_sem=s2.at[i - 1], recv_sem=r2.at[i - 1],
            device_id=(dst, me_w), device_id_type=MESH_ID,
        )

    for i in range(1, group):
        send2(i, me_g).start()
    for i in range(1, group):
        send2(i, lax.rem(me_g + group - i, group)).wait_recv()
    total = rc2[0].astype(jnp.float32)
    for i in range(1, group):
        total = total + rc2[i].astype(jnp.float32)
    out_ref[core, chip] = total.astype(jnp.bfloat16)

    def send3(i, slot):
        dst = lax.rem(chip + i, chips)
        return pltpu.make_async_remote_copy(
            src_ref=out_ref.at[core, slot], dst_ref=out_ref.at[core, slot],
            send_sem=s3.at[i - 1], recv_sem=r3.at[i - 1],
            device_id=(me_g, 2 * dst + core), device_id_type=MESH_ID,
        )

    def send4(side, slot, i):
        return pltpu.make_async_remote_copy(
            src_ref=out_ref.at[side, slot], dst_ref=out_ref.at[side, slot],
            send_sem=s4.at[i], recv_sem=r4.at[i],
            device_id=(me_g, mate), device_id_type=MESH_ID,
        )

    def go3(i, carry):
        send3(i, chip).start()
        return carry

    lax.fori_loop(1, chips, go3, 0)
    send4(core, chip, 0).start()

    def relay(i, carry):
        src = lax.rem(chip + chips - i, chips)
        send3(i, src).wait_recv()
        send4(core, src, i).start()
        return carry

    lax.fori_loop(1, chips, relay, 0)

    def finish(i, carry):
        src = lax.rem(chip + chips - i, chips)
        send4(1 - core, src, i).wait_recv()
        send4(core, src, i).wait_send()
        return carry

    lax.fori_loop(0, chips, finish, 0)

    def sent(i, carry):
        send1(i).wait_send()
        send3(i, chip).wait_send()
        return carry

    lax.fori_loop(1, chips, sent, 0)
    for i in range(1, group):
        send2(i, me_g).wait_send()


def per_device(vectors, centroids, list_ids, codes, rotation):
    rows, width = vectors.shape
    lists_local = centroids.shape[0]
    subspaces = codes.shape[1]
    sub_width = width // subspaces
    within = lax.axis_size("within")
    group = lax.axis_size("group")
    owned = subspaces // within
    high = owned * sub_width
    total_rows = rows * within * group
    chips = within // 2
    f32, bf16 = jnp.float32, jnp.bfloat16
    dma = pltpu.SemaphoreType.DMA

    local_list = list_ids % lists_local
    resid = (vectors.astype(f32) - jnp.take(centroids, local_list, axis=0)).astype(bf16)
    codes_t = codes.T
    rt = rotation.T.astype(bf16)

    def params(cid=None):
        if cid is None:
            return pltpu.CompilerParams(vmem_limit_bytes=VMEM_LIMIT)
        return pltpu.CompilerParams(
            vmem_limit_bytes=VMEM_LIMIT, collective_id=cid, has_side_effects=True
        )

    def local(kernel, msg_rows, ins):
        return pl.pallas_call(
            kernel,
            out_shape=(
                jax.ShapeDtypeStruct((within, msg_rows, HALF), f32),
                jax.ShapeDtypeStruct((8, width + HALF), f32),
            ),
            in_specs=[vmem_spec()] * len(ins),
            out_specs=(vmem_spec(), vmem_spec()),
            scratch_shapes=[pltpu.VMEM((width, rows), bf16), pltpu.VMEM((width, rows), bf16)],
            compiler_params=params(),
        )(*ins)

    def reduce_sums(last, cid, ins):
        msg_rows = ins[0].shape[1]
        outs = [
            jax.ShapeDtypeStruct((within, high, HALF), bf16),
            jax.ShapeDtypeStruct((8, width + HALF), f32),
        ]
        if last:
            outs += [jax.ShapeDtypeStruct((high, HALF), f32)] * 2
        else:
            outs += [jax.ShapeDtypeStruct((8, HALF), f32)]
        return pl.pallas_call(
            functools.partial(sums_kernel, within, group, last),
            out_shape=tuple(outs),
            in_specs=[vmem_spec()] * len(ins),
            out_specs=tuple([vmem_spec()] * len(outs)),
            scratch_shapes=[
                pltpu.VMEM((within - 1, msg_rows, HALF), f32),
                pltpu.VMEM((group, msg_rows, HALF), f32),
                dma, dma,
                dma((within - 1,)), dma((within - 1,)),
                dma((group - 1,)), dma((group - 1,)),
                dma((within - 1,)), dma((within - 1,)),
            ],
            compiler_params=params(cid),
        )(*ins)

    def rebuild(book, urow, other):
        return pl.pallas_call(
            recon_kernel,
            out_shape=jax.ShapeDtypeStruct((width, width), f32),
            in_specs=[vmem_spec()] * 5,
            out_specs=vmem_spec(),
            scratch_shapes=[pltpu.VMEM((width, rows), bf16), pltpu.VMEM((width, 8), f32)],
            compiler_params=params(),
        )(book, urow, other, codes_t, resid)

    def reduce_cross(cross, cid):
        block = (chips, width // chips, width // 2)
        return pl.pallas_call(
            functools.partial(cross_kernel, within, group),
            out_shape=jax.ShapeDtypeStruct((2,) + block, bf16),
            in_specs=[vmem_spec()],
            out_specs=vmem_spec(),
            scratch_shapes=[
                pltpu.VMEM(block, bf16),
                pltpu.VMEM(block, bf16),
                pltpu.VMEM((chips - 1,) + block[1:], bf16),
                pltpu.VMEM((group,) + block[1:], bf16),
                dma, dma,
                dma((chips - 1,)), dma((chips - 1,)),
                dma((group - 1,)), dma((group - 1,)),
                dma((chips - 1,)), dma((chips - 1,)),
                dma((chips,)), dma((chips,)),
            ],
            compiler_params=params(cid),
        )(cross)

    msg, urow = local(first_kernel, high + 8, (rt, resid, codes_t))
    book, other, counts = reduce_sums(False, 0, (msg, urow))
    cross = reduce_cross(rebuild(book, urow, other), 1)
    msg, urow = local(
        functools.partial(next_kernel, total_rows), 2 * high, (cross, resid, codes_t)
    )
    book, other, low, up = reduce_sums(True, 2, (msg, urow, counts))
    cross = reduce_cross(rebuild(book, urow, other), 3)
    rotated = pl.pallas_call(
        functools.partial(last_kernel, total_rows),
        out_shape=jax.ShapeDtypeStruct((rows, width), bf16),
        in_specs=[vmem_spec()] * 2,
        out_specs=vmem_spec(),
        compiler_params=params(),
    )(cross, resid)
    table = jnp.concatenate([low, up], axis=1).reshape(owned, sub_width, K)
    return rotated, table.transpose(0, 2, 1).reshape(owned, K * sub_width)


def solution(mesh):
    in_specs = (
        P(("group", "within"), None),
        P(("group", "within"), None),
        P(("group", "within")),
        P(("group", "within"), None),
        P(),
    )
    out_specs = (P(("group", "within"), None), P("within", None))
    return jax.shard_map(
        per_device, mesh=mesh, in_specs=in_specs, out_specs=out_specs, check_vma=False
    )
```

```python
import functools

import jax
import jax.numpy as jnp
from jax import lax
from jax.experimental import pallas as pl
from jax.experimental.pallas import tpu as pltpu
from jax.sharding import PartitionSpec as P

K = 256
HALF = K // 2
HOT = HALF + 16
ALTS = 2
NS_STEPS = 2
EPSILON = 1e-06
MESH_ID = pl.DeviceIdType.MESH
NT = (((1,), (1,)), ((), ()))
VMEM_LIMIT = 60 * 1024 * 1024
F32, BF16 = jnp.float32, jnp.bfloat16


def dot_nt(left, right):
    return lax.dot_general(left, right, NT, preferred_element_type=F32)


def dot(left, right):
    return jnp.dot(left, right, preferred_element_type=F32)


def polar(cross, total_rows):
    inv_rows = 1.0 / total_rows
    gram = dot_nt(cross, cross) * (inv_rows * inv_rows)
    norm_square = jnp.sqrt(jnp.sum(gram * gram) + EPSILON)
    inv_square = 1.0 / norm_square
    inv_scale = jnp.sqrt(inv_square)
    current = cross.astype(F32) * (inv_rows * inv_scale)
    gram = gram * inv_square
    for iteration in range(NS_STEPS):
        low = current.astype(BF16)
        if iteration > 0:
            gram = dot_nt(low, low)
        current = 1.5 * current - 0.5 * dot(gram.astype(BF16), low)
    return current.astype(BF16)


def whole_kernel(within, group, vec_ref, cen_ref, ids_ref, codes_in_ref, rotation_ref,
                 out_ref, low_ref, up_ref, *scratch):
    (resid_s, codes_s, rot_s, hot_s, urow_s, other_s, ucol_s, ccol_s, cnt_s, rec_s, own_s, rt_s,
     table_s, mate_t, plane_t, z_t, book_s, give_c, mate_c, plane_c, z_c, cross_s,
     pair_ss, pair_rs, mate_ss, mate_rs, plane_ss, plane_rs, z_ss, z_rs,
     back_ss, back_rs, relay_ss, relay_rs) = scratch
    rows, width = vec_ref.shape
    lists = cen_ref.shape[0]
    subspaces = codes_in_ref.shape[1]
    chips = within // 2
    total_rows = rows * within * group
    owned = subspaces // within
    high = 8 * owned
    me_g = lax.axis_index("group")
    me_w = lax.axis_index("within")
    core = lax.rem(me_w, 2)
    chip = me_w // 2
    other_core = 1 - core
    mate = (me_g, me_w + 1 - 2 * core)
    device = me_g * within + me_w
    wide = width // 2
    tall = width // chips

    def plane_peer(i):
        return (me_g, 2 * lax.rem(chip + i, chips) + core)

    def z_peer(i):
        return (lax.rem(me_g + i, group), me_w)

    def remote(src, dst, ss, rs, where):
        return pltpu.make_async_remote_copy(
            src_ref=src, dst_ref=dst, send_sem=ss, recv_sem=rs,
            device_id=where, device_id_type=MESH_ID,
        )

    def each(start, stop, body):
        def step(i, carry):
            body(i)
            return carry

        lax.fori_loop(start, stop, step, 0)

    barrier = pltpu.get_barrier_semaphore()
    pl.semaphore_signal(barrier, inc=1, device_id=mate, device_id_type=MESH_ID)
    each(1, chips, lambda i: pl.semaphore_signal(
        barrier, inc=1, device_id=plane_peer(i), device_id_type=MESH_ID))
    each(1, group, lambda i: pl.semaphore_signal(
        barrier, inc=1, device_id=z_peer(i), device_id_type=MESH_ID))

    local_list = jnp.broadcast_to(lax.rem(ids_ref[...], lists), (lists, rows))
    pick = jnp.where(lax.broadcasted_iota(jnp.int32, (lists, rows), 0) == local_list, 1.0, 0.0)
    pick = jnp.concatenate([pick, jnp.zeros((HALF - lists, rows), F32)], axis=0).T.astype(BF16)
    centre = cen_ref[...]
    pad = jnp.zeros((HALF - lists, width), F32)
    chosen = None
    for part in range(3):
        piece = centre.astype(BF16)
        centre = centre - piece.astype(F32)
        got = dot(pick, jnp.concatenate([piece.astype(F32), pad], axis=0).astype(BF16))
        chosen = got if chosen is None else chosen + got
    resid_s[...] = (vec_ref[...].astype(F32) - chosen).astype(BF16)

    wide_codes = jnp.concatenate(
        [codes_in_ref[...], jnp.zeros((rows, HALF - subspaces), jnp.int32)], axis=1
    )
    codes_s[...] = wide_codes.T

    urow_s[...] = jnp.zeros_like(urow_s)
    lane = lax.broadcasted_iota(jnp.int32, (1, HALF), 1)
    group_row = lax.broadcasted_iota(jnp.int32, (HALF, HALF), 0)
    lane_full = lax.broadcasted_iota(jnp.int32, (HALF, HALF), 1)

    def local_sums(alt):
        first = alt == 0
        levels = lax.broadcasted_iota(jnp.int32, (HOT, rows), 0)
        per_block = HALF // 8

        def block(b, counts):
            at = pl.multiple_of(b * HALF, HALF)
            right = rot_s[:, pl.ds(at, HALF)]
            if first:
                right = jnp.concatenate([right, jnp.ones((rows, HALF), BF16)], axis=1)
            total = jnp.zeros((HOT, HALF), F32)
            for i in range(per_block):
                m = b * per_block + i
                if first:
                    code = jnp.minimum(codes_s[pl.ds(m, 1), :], HALF)
                    hot = jnp.where(levels == code, 1.0, 0.0).astype(BF16)
                    hot_s[m] = hot
                else:
                    hot = hot_s[m]
                out = dot(hot, right)
                here = (lane >= 8 * i) & (lane < 8 * i + 8)
                total = jnp.where(here, out[:, 0:HALF], total)
                if first:
                    counts = jnp.where(lane == m, out[:, HALF : 2 * HALF], counts)
            flipped = total[0:HALF].T
            for i in range(per_block):
                m = b * per_block + i
                w = m // owned
                spot = pl.multiple_of(8 * (m - w * owned), 8)
                table_s[alt, w // 2, lax.rem(w, 2), pl.ds(spot, 8), :] = flipped[8 * i : 8 * i + 8]
            urow_s[alt, pl.ds(b, 1), :] = total[HALF : HALF + 1]
            return counts

        counts = lax.fori_loop(0, width // HALF, block, jnp.zeros((HOT, HALF), F32))
        if first:
            urow_s[0, pl.ds(width // HALF, 1), :] = counts[HALF : HALF + 1]
            rec_c = counts[0:HALF].T
            upper = jnp.broadcast_to(urow_s[0].T[:, width // HALF : width // HALF + 1], (HALF, HALF))
            upper = jnp.where(lane_full == lax.rem(device + group_row, HALF), upper, 0.0)
            for w in range(within):
                for i in range(owned):
                    m = w * owned + i
                    table_s[0, w // 2, w % 2, high + i : high + i + 1, :] = rec_c[m : m + 1]
                    table_s[0, w // 2, w % 2, high + owned + i : high + owned + i + 1, :] = upper[
                        m : m + 1
                    ]
        else:
            columns = urow_s[alt].T
            for b in range(width // HALF):
                upper = jnp.broadcast_to(columns[:, b : b + 1], (HALF, HALF))
                spot = lax.rem(device + b * per_block + group_row // 8, HALF)
                upper = jnp.where(lane_full == spot, upper, 0.0)
                for i in range(per_block):
                    m = b * per_block + i
                    w = m // owned
                    at = high + 8 * (m % owned)
                    table_s[alt, w // 2, w % 2, at : at + 8, :] = upper[8 * i : 8 * i + 8]

    def reduce_sums(alt):
        size = high + 8 if alt == 0 else 2 * high
        span = pl.ds(0, size)
        give = remote(table_s.at[alt, :, other_core, span, :], mate_t.at[alt, :, span, :],
                      mate_ss.at[0, alt], mate_rs.at[0, alt], mate)
        give.start()
        swap = remote(urow_s.at[alt], other_s.at[alt], pair_ss.at[alt], pair_rs.at[alt],
                      z_peer(group // 2))
        swap.start()
        give.wait()

        def out1(i):
            return remote(table_s.at[alt, lax.rem(chip + i, chips), core, span, :],
                          plane_t.at[alt, i - 1, span, :],
                          plane_ss.at[0, alt, i - 1], plane_rs.at[0, alt, i - 1], plane_peer(i))

        def go1(i):
            to = lax.rem(chip + i, chips)
            table_s[alt, to, core, span, :] = (
                table_s[alt, to, core, span, :] + mate_t[alt, to, span, :]
            )
            out1(i).start()

        each(1, chips, go1)

        def take1(i, acc):
            out1(i).wait_recv()
            return acc + plane_t[alt, i - 1, span, :]

        acc = table_s[alt, chip, core, span, :] + mate_t[alt, chip, span, :]
        z_t[alt, me_g, span, :] = lax.fori_loop(1, chips, take1, acc)

        def out2(i, slot):
            return remote(z_t.at[alt, slot, span, :], z_t.at[alt, slot, span, :],
                          z_ss.at[0, alt, i - 1], z_rs.at[0, alt, i - 1], z_peer(i))

        each(1, group, lambda i: out2(i, me_g).start())
        each(1, group, lambda i: out2(i, lax.rem(me_g + group - i, group)).wait_recv())
        total = z_t[alt, 0, span, :]
        for g in range(1, group):
            total = total + z_t[alt, g, span, :]
        if alt == 0:
            cnt_s[...] = total[high : high + 8] + 1.0
        counts = cnt_s[...]
        low = jnp.concatenate(
            [total[8 * i : 8 * i + 8] / counts[i : i + 1] for i in range(owned)], axis=0
        )
        book_s[alt, core, chip] = low.astype(BF16)

        def out3(i, slot):
            return remote(book_s.at[alt, core, slot], book_s.at[alt, core, slot],
                          back_ss.at[0, alt, i - 1], back_rs.at[0, alt, i - 1], plane_peer(i))

        def out4(side, slot, i):
            return remote(book_s.at[alt, side, slot], book_s.at[alt, side, slot],
                          relay_ss.at[0, alt, i], relay_rs.at[0, alt, i], mate)

        each(1, chips, lambda i: out3(i, chip).start())
        out4(core, chip, 0).start()
        if alt == ALTS - 1:
            low_ref[...] = low
            up_ref[...] = jnp.concatenate(
                [total[high + 8 * i : high + 8 * i + 8] / counts[owned + i : owned + i + 1]
                 for i in range(owned)], axis=0,
            )
        swap.wait()
        columns = (urow_s[alt] + other_s[alt]).T
        for b in range(width // HALF):
            ucol_s[b * HALF : b * HALF + HALF, :] = jnp.broadcast_to(
                columns[:, b : b + 1], (HALF, HALF)
            )
        if alt == 0:
            at = width // HALF
            ccol_s[...] = jnp.broadcast_to(columns[:, at : at + 1], (HALF, HALF)) + 1.0

        def relay(i):
            src = lax.rem(chip + chips - i, chips)
            out3(i, src).wait_recv()
            out4(core, src, i).start()

        each(1, chips, relay)

        def finish(i):
            src = lax.rem(chip + chips - i, chips)
            out4(other_core, src, i).wait_recv()
            out4(core, src, i).wait_send()

        each(0, chips, finish)

        def sent(i):
            out1(i).wait_send()
            out3(i, chip).wait_send()

        each(1, chips, sent)
        each(1, group, lambda i: out2(i, me_g).wait_send())

    def rebuild(alt):
        def step(at, carry):
            table = jnp.concatenate([book_s[alt, 0, at], book_s[alt, 1, at]], axis=0).astype(F32)
            for pair in range(owned):
                pieces = []
                for sub in range(2):
                    local = 2 * pair + sub
                    m = at * (2 * owned) + local
                    words = table[8 * local : 8 * local + 8, :]
                    column = ucol_s[pl.ds(pl.multiple_of(8 * m, 8), 8), :] / ccol_s[pl.ds(m, 1), :]
                    row_pieces = []
                    code_row = codes_s[pl.ds(m, 1), :]
                    for part in range(rows // HALF):
                        code = jnp.broadcast_to(
                            code_row[:, HALF * part : HALF * part + HALF], (8, HALF)
                        )
                        low = jnp.take_along_axis(
                            words, jnp.bitwise_and(code, HALF - 1), axis=1,
                            mode="promise_in_bounds",
                        )
                        row_pieces.append(jnp.where(code >= HALF, column, low))
                    pieces.append(jnp.concatenate(row_pieces, axis=1))
                spot = pl.multiple_of(at * 16 * owned + 16 * pair, 16)
                rec_s[pl.ds(spot, 16), :] = jnp.concatenate(pieces, axis=0).astype(BF16)
            return carry

        lax.fori_loop(0, chips, step, 0)

    def reduce_cross(alt):
        mate_at = pl.multiple_of(other_core * wide, wide)
        mine_at = pl.multiple_of(core * wide, wide)
        give_c[alt, 0] = dot(rec_s[...], resid_s[:, pl.ds(mate_at, wide)]).astype(BF16).reshape(
            chips, tall, wide
        )
        give = remote(give_c.at[alt, 0], mate_c.at[alt],
                      mate_ss.at[1, alt], mate_rs.at[1, alt], mate)
        give.start()
        own_s[...] = dot(rec_s[...], resid_s[:, pl.ds(mine_at, wide)]).reshape(chips, tall, wide)
        give.wait_recv()

        def out1(i):
            return remote(give_c.at[alt, 1, lax.rem(chip + i, chips)], plane_c.at[alt, i - 1],
                          plane_ss.at[1, alt, i - 1], plane_rs.at[1, alt, i - 1], plane_peer(i))

        def go1(i):
            to = lax.rem(chip + i, chips)
            give_c[alt, 1, to] = (own_s[to] + mate_c[alt, to].astype(F32)).astype(BF16)
            out1(i).start()

        each(1, chips, go1)

        def take1(i, acc):
            out1(i).wait_recv()
            return acc + plane_c[alt, i - 1].astype(F32)

        acc = own_s[chip] + mate_c[alt, chip].astype(F32)
        z_c[alt, me_g] = lax.fori_loop(1, chips, take1, acc).astype(BF16)

        def out2(i, slot):
            return remote(z_c.at[alt, slot], z_c.at[alt, slot],
                          z_ss.at[1, alt, i - 1], z_rs.at[1, alt, i - 1], z_peer(i))

        each(1, group, lambda i: out2(i, me_g).start())
        each(1, group, lambda i: out2(i, lax.rem(me_g + group - i, group)).wait_recv())
        total = z_c[alt, 0].astype(F32)
        for g in range(1, group):
            total = total + z_c[alt, g].astype(F32)
        cross_s[alt, core, chip] = total.astype(BF16)

        def out3(i, slot):
            return remote(cross_s.at[alt, core, slot], cross_s.at[alt, core, slot],
                          back_ss.at[1, alt, i - 1], back_rs.at[1, alt, i - 1], plane_peer(i))

        def out4(side, slot, i):
            return remote(cross_s.at[alt, side, slot], cross_s.at[alt, side, slot],
                          relay_ss.at[1, alt, i], relay_rs.at[1, alt, i], mate)

        each(1, chips, lambda i: out3(i, chip).start())
        out4(core, chip, 0).start()

        def relay(i):
            src = lax.rem(chip + chips - i, chips)
            out3(i, src).wait_recv()
            out4(core, src, i).start()

        each(1, chips, relay)

        def finish(i):
            src = lax.rem(chip + chips - i, chips)
            out4(other_core, src, i).wait_recv()
            out4(core, src, i).wait_send()

        each(0, chips, finish)

        def sent(i):
            out1(i).wait_send()
            out3(i, chip).wait_send()

        each(1, chips, sent)
        each(1, group, lambda i: out2(i, me_g).wait_send())
        give.wait_send()

    for alt in range(ALTS):
        if alt == 0:
            rot_s[...] = dot(resid_s[...], rotation_ref[...].astype(BF16)).astype(BF16)
        else:
            rot_s[...] = dot_nt(resid_s[...], rt_s[...]).astype(BF16)
        local_sums(alt)
        if alt == 0:
            pl.semaphore_wait(barrier, chips + group - 1)
        reduce_sums(alt)
        rebuild(alt)
        reduce_cross(alt)
        halves = [cross_s[alt, side].reshape(width, wide) for side in range(2)]
        rt_s[...] = polar(jnp.concatenate(halves, axis=1), total_rows)
    out_ref[...] = dot_nt(resid_s[...], rt_s[...]).astype(BF16)


def per_device(vectors, centroids, list_ids, codes, rotation):
    rows, width = vectors.shape
    subspaces = codes.shape[1]
    sub_width = width // subspaces
    within = lax.axis_size("within")
    group = lax.axis_size("group")
    owned = subspaces // within
    high = owned * sub_width
    chips = within // 2
    block = (width // chips, width // 2)
    dma = pltpu.SemaphoreType.DMA
    vmem = pl.BlockSpec(memory_space=pltpu.VMEM)
    scratch = [
        pltpu.VMEM((rows, width), BF16),
        pltpu.VMEM((HALF, rows), jnp.int32),
        pltpu.VMEM((rows, width), BF16),
        pltpu.VMEM((subspaces, HOT, rows), BF16),
        pltpu.VMEM((ALTS, 8, HALF), F32),
        pltpu.VMEM((ALTS, 8, HALF), F32),
        pltpu.VMEM((width, HALF), F32),
        pltpu.VMEM((HALF, HALF), F32),
        pltpu.VMEM((8, HALF), F32),
        pltpu.VMEM((width, rows), BF16),
        pltpu.VMEM((chips,) + block, F32),
        pltpu.VMEM((width, width), BF16),
        pltpu.VMEM((ALTS, chips, 2, 2 * high, HALF), F32),
        pltpu.VMEM((ALTS, chips, 2 * high, HALF), F32),
        pltpu.VMEM((ALTS, chips - 1, 2 * high, HALF), F32),
        pltpu.VMEM((ALTS, group, 2 * high, HALF), F32),
        pltpu.VMEM((ALTS, 2, chips, high, HALF), BF16),
        pltpu.VMEM((ALTS, 2, chips) + block, BF16),
        pltpu.VMEM((ALTS, chips) + block, BF16),
        pltpu.VMEM((ALTS, chips - 1) + block, BF16),
        pltpu.VMEM((ALTS, group) + block, BF16),
        pltpu.VMEM((ALTS, 2, chips) + block, BF16),
        dma((ALTS,)), dma((ALTS,)),
        dma((2, ALTS)), dma((2, ALTS)),
        dma((2, ALTS, chips - 1)), dma((2, ALTS, chips - 1)),
        dma((2, ALTS, group - 1)), dma((2, ALTS, group - 1)),
        dma((2, ALTS, chips - 1)), dma((2, ALTS, chips - 1)),
        dma((2, ALTS, chips)), dma((2, ALTS, chips)),
    ]
    rotated, low, up = pl.pallas_call(
        functools.partial(whole_kernel, within, group),
        out_shape=(
            jax.ShapeDtypeStruct((rows, width), BF16),
            jax.ShapeDtypeStruct((high, HALF), F32),
            jax.ShapeDtypeStruct((high, HALF), F32),
        ),
        in_specs=[vmem] * 5,
        out_specs=(vmem, vmem, vmem),
        scratch_shapes=scratch,
        compiler_params=pltpu.CompilerParams(
            vmem_limit_bytes=VMEM_LIMIT, collective_id=0, has_side_effects=True
        ),
    )(vectors, centroids, list_ids.reshape(1, rows), codes, rotation)
    table = jnp.concatenate([low, up], axis=1).reshape(owned, sub_width, K)
    return rotated, table.transpose(0, 2, 1).reshape(owned, K * sub_width)


def solution(mesh):
    in_specs = (
        P(("group", "within"), None),
        P(("group", "within"), None),
        P(("group", "within")),
        P(("group", "within"), None),
        P(),
    )
    out_specs = (P(("group", "within"), None), P("within", None))
    return jax.shard_map(
        per_device, mesh=mesh, in_specs=in_specs, out_specs=out_specs, check_vma=False
    )
```

```python
import functools

import jax
import jax.numpy as jnp
from jax import lax
from jax.experimental import pallas as pl
from jax.experimental.pallas import tpu as pltpu
from jax.sharding import PartitionSpec as P

K = 256
HALF = K // 2
HOT = HALF + 16
ALTS = 2
NS_STEPS = 2
EPSILON = 1e-06
CUTS = ((0, 256), (256, 128))
MESH_ID = pl.DeviceIdType.MESH
NT = (((1,), (1,)), ((), ()))
VMEM_LIMIT = 60 * 1024 * 1024
F32, BF16 = jnp.float32, jnp.bfloat16


def dot_nt(left, right):
    return lax.dot_general(left, right, NT, preferred_element_type=F32)


def dot(left, right):
    return jnp.dot(left, right, preferred_element_type=F32)


def polar(cross, gram, total_rows):
    inv_rows = 1.0 / total_rows
    gram = gram * (inv_rows * inv_rows)
    norm_square = jnp.sqrt(jnp.sum(gram * gram) + EPSILON)
    inv_square = 1.0 / norm_square
    inv_scale = jnp.sqrt(inv_square)
    current = cross.astype(F32) * (inv_rows * inv_scale)
    gram = gram * inv_square
    for iteration in range(NS_STEPS):
        low = current.astype(BF16)
        if iteration > 0:
            gram = dot_nt(low, low)
        current = 1.5 * current - 0.5 * dot(gram.astype(BF16), low)
    return current.astype(BF16)


def split_count(count):
    upper = jnp.floor(count * (1.0 / 256.0))
    return count - 256.0 * upper, upper


def whole_kernel(within, group, vec_ref, cen_ref, ids_ref, codes_s, rotation_ref,
                 out_ref, low_ref, up_ref, *scratch):
    (resid_s, rot_s, hot_s, urow_s, other_s, ucol_s, ccol_s, cnt_s, rec_s, rt_s,
     table_s, mate_t, send_t, plane_t, z_t, book_s,
     pair_ss, pair_rs, mate_ss, mate_rs, plane_ss, plane_rs, z_ss, z_rs,
     back_ss, back_rs, relay_ss, relay_rs) = scratch[:28]
    pieces_c = [scratch[28 + 6 * c : 34 + 6 * c] for c in range(len(CUTS))]
    rows, width = vec_ref.shape
    lists = cen_ref.shape[0]
    subspaces = codes_s.shape[0]
    chips = within // 2
    side = 4
    total_rows = rows * within * group
    owned = subspaces // within
    high = 8 * owned
    me_g = lax.axis_index("group")
    me_w = lax.axis_index("within")
    core = lax.rem(me_w, 2)
    chip = me_w // 2
    chip_y, chip_x = chip // side, lax.rem(chip, side)
    other_core = 1 - core
    mate = (me_g, me_w + 1 - 2 * core)
    device = me_g * within + me_w
    wide = width // 2
    tall = width // chips

    def offset(i):
        at = lax.rem(5 * i, chips)
        return at // side, lax.rem(at, side)

    def chip_to(i):
        y, x = offset(i)
        return lax.rem(chip_y + y, side) * side + lax.rem(chip_x + x, side)

    def chip_from(i):
        y, x = offset(i)
        return lax.rem(chip_y + side - y, side) * side + lax.rem(chip_x + side - x, side)

    def plane_peer(i):
        return (me_g, 2 * chip_to(i) + core)

    def z_from(i):
        return lax.rem(me_g + group - lax.rem(3 * i, group), group)

    def z_peer(i):
        return (lax.rem(me_g + lax.rem(3 * i, group), group), me_w)

    def remote(src, dst, ss, rs, where):
        return pltpu.make_async_remote_copy(
            src_ref=src, dst_ref=dst, send_sem=ss, recv_sem=rs,
            device_id=where, device_id_type=MESH_ID,
        )

    def each(start, stop, body):
        def step(i, carry):
            body(i)
            return carry

        lax.fori_loop(start, stop, step, 0)

    barrier = pltpu.get_barrier_semaphore()
    pl.semaphore_signal(barrier, inc=1, device_id=mate, device_id_type=MESH_ID)
    each(1, chips, lambda i: pl.semaphore_signal(
        barrier, inc=1, device_id=plane_peer(i), device_id_type=MESH_ID))
    each(1, group, lambda i: pl.semaphore_signal(
        barrier, inc=1, device_id=z_peer(i), device_id_type=MESH_ID))

    local_list = jnp.broadcast_to(lax.rem(ids_ref[...], lists), (lists, rows))
    pick = jnp.where(lax.broadcasted_iota(jnp.int32, (lists, rows), 0) == local_list, 1.0, 0.0)
    pick = jnp.concatenate([pick, jnp.zeros((HALF - lists, rows), F32)], axis=0).T.astype(BF16)
    centre = cen_ref[...]
    pad = jnp.zeros((HALF - lists, width), F32)
    chosen = None
    for part in range(3):
        piece = centre.astype(BF16)
        centre = centre - piece.astype(F32)
        got = dot(pick, jnp.concatenate([piece.astype(F32), pad], axis=0).astype(BF16))
        chosen = got if chosen is None else chosen + got
    resid_s[...] = (vec_ref[...].astype(F32) - chosen).astype(BF16)

    urow_s[...] = jnp.zeros_like(urow_s)
    lane = lax.broadcasted_iota(jnp.int32, (1, HALF), 1)
    group_row = lax.broadcasted_iota(jnp.int32, (HALF, HALF), 0)
    lane_full = lax.broadcasted_iota(jnp.int32, (HALF, HALF), 1)

    def local_sums(alt):
        first = alt == 0
        levels = lax.broadcasted_iota(jnp.int32, (HOT, rows), 0)
        per_block = HALF // 8

        def block(b, counts):
            at = pl.multiple_of(b * HALF, HALF)
            right = rot_s[:, pl.ds(at, HALF)]
            if first:
                right = jnp.concatenate([right, jnp.ones((rows, HALF), BF16)], axis=1)
            total = jnp.zeros((HOT, HALF), F32)
            for i in range(per_block):
                m = b * per_block + i
                if first:
                    code = jnp.minimum(codes_s[pl.ds(m, 1), :], HALF)
                    hot = jnp.where(levels == code, 1.0, 0.0).astype(BF16)
                    hot_s[m] = hot
                else:
                    hot = hot_s[m]
                out = dot(hot, right)
                here = (lane >= 8 * i) & (lane < 8 * i + 8)
                total = jnp.where(here, out[:, 0:HALF], total)
                if first:
                    counts = jnp.where(lane == m, out[:, HALF : 2 * HALF], counts)
            flipped = total[0:HALF].T
            for i in range(per_block):
                m = b * per_block + i
                w = m // owned
                spot = pl.multiple_of(8 * (m - w * owned), 8)
                table_s[alt, w // 2, lax.rem(w, 2), pl.ds(spot, 8), :] = flipped[8 * i : 8 * i + 8]
            urow_s[alt, pl.ds(b, 1), :] = total[HALF : HALF + 1]
            return counts

        counts = lax.fori_loop(0, width // HALF, block, jnp.zeros((HOT, HALF), F32))
        if first:
            urow_s[0, pl.ds(width // HALF, 1), :] = counts[HALF : HALF + 1]
            rec_c = counts[0:HALF].T
            upper = jnp.broadcast_to(urow_s[0].T[:, width // HALF : width // HALF + 1], (HALF, HALF))
            upper = jnp.where(lane_full == lax.rem(device + group_row, HALF), upper, 0.0)
            for w in range(within):
                for i in range(owned):
                    m = w * owned + i
                    table_s[0, w // 2, w % 2, high + i : high + i + 1, :] = rec_c[m : m + 1]
                    table_s[0, w // 2, w % 2, high + owned + i : high + owned + i + 1, :] = upper[
                        m : m + 1
                    ]
        else:
            columns = urow_s[alt].T
            for b in range(width // HALF):
                upper = jnp.broadcast_to(columns[:, b : b + 1], (HALF, HALF))
                spot = lax.rem(device + b * per_block + group_row // 8, HALF)
                upper = jnp.where(lane_full == spot, upper, 0.0)
                for i in range(per_block):
                    m = b * per_block + i
                    w = m // owned
                    at = high + 8 * (m % owned)
                    table_s[alt, w // 2, w % 2, at : at + 8, :] = upper[8 * i : 8 * i + 8]

    def reduce_sums(alt):
        size = high + 8 if alt == 0 else 2 * high
        sent = high + 16 if alt == 0 else 2 * high
        span = pl.ds(0, size)
        span16 = pl.ds(0, sent)

        def pack(part):
            if alt > 0:
                return part.astype(BF16)
            less, more = split_count(part[high : high + 8])
            return jnp.concatenate([part[0:high], less, more], axis=0).astype(BF16)

        def unpack(part):
            part = part.astype(F32)
            if alt > 0:
                return part
            count = part[high : high + 8] + 256.0 * part[high + 8 : high + 16]
            return jnp.concatenate([part[0:high], count], axis=0)

        give = remote(table_s.at[alt, :, other_core, span, :], mate_t.at[alt, :, span, :],
                      mate_ss.at[0, alt], mate_rs.at[0, alt], mate)
        give.start()
        swap = remote(urow_s.at[alt], other_s.at[alt], pair_ss.at[alt], pair_rs.at[alt],
                      (lax.rem(me_g + group // 2, group), me_w))
        swap.start()
        give.wait()

        def out1(i):
            return remote(send_t.at[alt, chip_to(i), span16, :],
                          plane_t.at[alt, i - 1, span16, :],
                          plane_ss.at[0, alt, i - 1], plane_rs.at[0, alt, i - 1], plane_peer(i))

        def go1(i):
            to = chip_to(i)
            send_t[alt, to, span16, :] = pack(
                table_s[alt, to, core, span, :] + mate_t[alt, to, span, :]
            )
            out1(i).start()

        each(1, chips, go1)

        def take1(i, acc):
            out1(i).wait_recv()
            return acc + unpack(plane_t[alt, i - 1, span16, :])

        acc = table_s[alt, chip, core, span, :] + mate_t[alt, chip, span, :]
        z_t[alt, me_g, span16, :] = pack(lax.fori_loop(1, chips, take1, acc))

        def out2(i, slot):
            return remote(z_t.at[alt, slot, span16, :], z_t.at[alt, slot, span16, :],
                          z_ss.at[0, alt, i - 1], z_rs.at[0, alt, i - 1], z_peer(i))

        each(1, group, lambda i: out2(i, me_g).start())
        swap.wait()
        columns = (urow_s[alt] + other_s[alt]).T
        for b in range(width // HALF):
            ucol_s[b * HALF : b * HALF + HALF, :] = jnp.broadcast_to(
                columns[:, b : b + 1], (HALF, HALF)
            )
        if alt == 0:
            at = width // HALF
            ccol_s[...] = jnp.broadcast_to(columns[:, at : at + 1], (HALF, HALF)) + 1.0
        each(1, group, lambda i: out2(i, z_from(i)).wait_recv())
        total = unpack(z_t[alt, 0, span16, :])
        for g in range(1, group):
            total = total + unpack(z_t[alt, g, span16, :])
        if alt == 0:
            cnt_s[...] = total[high : high + 8] + 1.0
        counts = cnt_s[...]
        low = jnp.concatenate(
            [total[8 * i : 8 * i + 8] / counts[i : i + 1] for i in range(owned)], axis=0
        )
        book_s[alt, core, chip] = low.astype(BF16)

        def out3(i, slot):
            return remote(book_s.at[alt, core, slot], book_s.at[alt, core, slot],
                          back_ss.at[0, alt, i - 1], back_rs.at[0, alt, i - 1], plane_peer(i))

        def out4(half, slot, i):
            return remote(book_s.at[alt, half, slot], book_s.at[alt, half, slot],
                          relay_ss.at[0, alt, i], relay_rs.at[0, alt, i], mate)

        each(1, chips, lambda i: out3(i, chip).start())
        out4(core, chip, 0).start()
        if alt == ALTS - 1:
            low_ref[...] = low
            up_ref[...] = jnp.concatenate(
                [total[high + 8 * i : high + 8 * i + 8] / counts[owned + i : owned + i + 1]
                 for i in range(owned)], axis=0,
            )

        def relay(i):
            src = chip_from(i)
            out3(i, src).wait_recv()
            out4(core, src, i).start()

        each(1, chips, relay)

        def finish(i):
            src = chip_from(i)
            out4(other_core, src, i).wait_recv()
            out4(core, src, i).wait_send()

        each(0, chips, finish)

        def gone(i):
            out1(i).wait_send()
            out3(i, chip).wait_send()

        each(1, chips, gone)
        each(1, group, lambda i: out2(i, me_g).wait_send())

    def rebuild(alt):
        def step(at, carry):
            table = jnp.concatenate([book_s[alt, 0, at], book_s[alt, 1, at]], axis=0).astype(F32)
            for pair in range(owned):
                pieces = []
                for sub in range(2):
                    local = 2 * pair + sub
                    m = at * (2 * owned) + local
                    words = table[8 * local : 8 * local + 8, :]
                    column = ucol_s[pl.ds(pl.multiple_of(8 * m, 8), 8), :] / ccol_s[pl.ds(m, 1), :]
                    row_pieces = []
                    code_row = codes_s[pl.ds(m, 1), :]
                    for part in range(rows // HALF):
                        code = jnp.broadcast_to(
                            code_row[:, HALF * part : HALF * part + HALF], (8, HALF)
                        )
                        low = jnp.take_along_axis(
                            words, jnp.bitwise_and(code, HALF - 1), axis=1,
                            mode="promise_in_bounds",
                        )
                        row_pieces.append(jnp.where(code >= HALF, column, low))
                    pieces.append(jnp.concatenate(row_pieces, axis=1))
                spot = pl.multiple_of(at * 16 * owned + 16 * pair, 16)
                rec_s[pl.ds(spot, 16), :] = jnp.concatenate(pieces, axis=0).astype(BF16)
            return carry

        lax.fori_loop(0, chips, step, 0)

    def reduce_cross(alt):
        gives = []
        for c, (start, size) in enumerate(CUTS):
            give_c, mate_c = pieces_c[c][0], pieces_c[c][1]
            at = pl.multiple_of(other_core * wide + start, HALF)
            give_c[alt, 0] = dot(rec_s[...], resid_s[:, pl.ds(at, size)]).astype(BF16).reshape(
                chips, tall, size
            )
            give = remote(give_c.at[alt, 0], mate_c.at[alt],
                          mate_ss.at[1 + c, alt], mate_rs.at[1 + c, alt], mate)
            give.start()
            gives.append(give)

        def out1(c, i):
            give_c, plane_c = pieces_c[c][0], pieces_c[c][2]
            return remote(give_c.at[alt, 1, chip_to(i)], plane_c.at[alt, i - 1],
                          plane_ss.at[1 + c, alt, i - 1], plane_rs.at[1 + c, alt, i - 1],
                          plane_peer(i))

        def out2(c, i, slot):
            z_c = pieces_c[c][3]
            return remote(z_c.at[alt, slot], z_c.at[alt, slot],
                          z_ss.at[1 + c, alt, i - 1], z_rs.at[1 + c, alt, i - 1], z_peer(i))

        def out3(c, i, slot):
            cross_s = pieces_c[c][4]
            return remote(cross_s.at[alt, core, slot], cross_s.at[alt, core, slot],
                          back_ss.at[1 + c, alt, i - 1], back_rs.at[1 + c, alt, i - 1],
                          plane_peer(i))

        def out4(c, half, slot, i):
            cross_s = pieces_c[c][4]
            return remote(cross_s.at[alt, half, slot], cross_s.at[alt, half, slot],
                          relay_ss.at[1 + c, alt, i], relay_rs.at[1 + c, alt, i], mate)

        for c, (start, size) in enumerate(CUTS):
            give_c, mate_c, own_c = pieces_c[c][0], pieces_c[c][1], pieces_c[c][5]
            at = pl.multiple_of(core * wide + start, HALF)
            own_c[...] = dot(rec_s[...], resid_s[:, pl.ds(at, size)]).reshape(chips, tall, size)
            gives[c].wait_recv()

            def go1(i):
                to = chip_to(i)
                give_c[alt, 1, to] = (own_c[to] + mate_c[alt, to].astype(F32)).astype(BF16)
                out1(c, i).start()

            each(1, chips, go1)
        for c in range(len(CUTS)):
            mate_c, plane_c, z_c, own_c = (pieces_c[c][k] for k in (1, 2, 3, 5))

            def take1(i, acc):
                out1(c, i).wait_recv()
                return acc + plane_c[alt, i - 1].astype(F32)

            acc = own_c[chip] + mate_c[alt, chip].astype(F32)
            z_c[alt, me_g] = lax.fori_loop(1, chips, take1, acc).astype(BF16)
            each(1, group, lambda i: out2(c, i, me_g).start())
        for c in range(len(CUTS)):
            z_c, cross_s = pieces_c[c][3], pieces_c[c][4]
            each(1, group, lambda i: out2(c, i, z_from(i)).wait_recv())
            total = z_c[alt, 0].astype(F32)
            for g in range(1, group):
                total = total + z_c[alt, g].astype(F32)
            cross_s[alt, core, chip] = total.astype(BF16)
            each(1, chips, lambda i: out3(c, i, chip).start())
            out4(c, core, chip, 0).start()
        gram = None
        for c, (start, size) in enumerate(CUTS):
            cross_s = pieces_c[c][4]

            def relay(i):
                src = chip_from(i)
                out3(c, i, src).wait_recv()
                out4(c, core, src, i).start()

            each(1, chips, relay)

            def finish(i):
                src = chip_from(i)
                out4(c, other_core, src, i).wait_recv()
                out4(c, core, src, i).wait_send()

            each(0, chips, finish)
            part = jnp.concatenate(
                [cross_s[alt, half].reshape(width, size) for half in range(2)], axis=1
            )
            part = dot_nt(part, part)
            gram = part if gram is None else gram + part
        for c in range(len(CUTS)):

            def gone(i):
                out1(c, i).wait_send()
                out3(c, i, chip).wait_send()

            each(1, chips, gone)
            each(1, group, lambda i: out2(c, i, me_g).wait_send())
            gives[c].wait_send()
        whole = jnp.concatenate(
            [pieces_c[c][4][alt, half].reshape(width, CUTS[c][1])
             for half in range(2) for c in range(len(CUTS))], axis=1,
        )
        rt_s[...] = polar(whole, gram, total_rows)

    for alt in range(ALTS):
        if alt == 0:
            rot_s[...] = dot(resid_s[...], rotation_ref[...].astype(BF16)).astype(BF16)
        else:
            rot_s[...] = dot_nt(resid_s[...], rt_s[...]).astype(BF16)
        local_sums(alt)
        if alt == 0:
            pl.semaphore_wait(barrier, chips + group - 1)
        reduce_sums(alt)
        rebuild(alt)
        reduce_cross(alt)
    out_ref[...] = dot_nt(resid_s[...], rt_s[...]).astype(BF16)


def per_device(vectors, centroids, list_ids, codes, rotation):
    rows, width = vectors.shape
    subspaces = codes.shape[1]
    sub_width = width // subspaces
    within = lax.axis_size("within")
    group = lax.axis_size("group")
    owned = subspaces // within
    high = owned * sub_width
    chips = within // 2
    dma = pltpu.SemaphoreType.DMA
    vmem = pl.BlockSpec(memory_space=pltpu.VMEM)
    kinds = 1 + len(CUTS)
    scratch = [
        pltpu.VMEM((rows, width), BF16),
        pltpu.VMEM((rows, width), BF16),
        pltpu.VMEM((subspaces, HOT, rows), BF16),
        pltpu.VMEM((ALTS, 8, HALF), F32),
        pltpu.VMEM((ALTS, 8, HALF), F32),
        pltpu.VMEM((width, HALF), F32),
        pltpu.VMEM((HALF, HALF), F32),
        pltpu.VMEM((8, HALF), F32),
        pltpu.VMEM((width, rows), BF16),
        pltpu.VMEM((width, width), BF16),
        pltpu.VMEM((ALTS, chips, 2, 2 * high, HALF), F32),
        pltpu.VMEM((ALTS, chips, 2 * high, HALF), F32),
        pltpu.VMEM((ALTS, chips, 2 * high, HALF), BF16),
        pltpu.VMEM((ALTS, chips - 1, 2 * high, HALF), BF16),
        pltpu.VMEM((ALTS, group, 2 * high, HALF), BF16),
        pltpu.VMEM((ALTS, 2, chips, high, HALF), BF16),
        dma((ALTS,)), dma((ALTS,)),
        dma((kinds, ALTS)), dma((kinds, ALTS)),
        dma((kinds, ALTS, chips - 1)), dma((kinds, ALTS, chips - 1)),
        dma((kinds, ALTS, group - 1)), dma((kinds, ALTS, group - 1)),
        dma((kinds, ALTS, chips - 1)), dma((kinds, ALTS, chips - 1)),
        dma((kinds, ALTS, chips)), dma((kinds, ALTS, chips)),
    ]
    for start, size in CUTS:
        block = (width // chips, size)
        scratch += [
            pltpu.VMEM((ALTS, 2, chips) + block, BF16),
            pltpu.VMEM((ALTS, chips) + block, BF16),
            pltpu.VMEM((ALTS, chips - 1) + block, BF16),
            pltpu.VMEM((ALTS, group) + block, BF16),
            pltpu.VMEM((ALTS, 2, chips) + block, BF16),
            pltpu.VMEM((chips,) + block, F32),
        ]
    rotated, low, up = pl.pallas_call(
        functools.partial(whole_kernel, within, group),
        out_shape=(
            jax.ShapeDtypeStruct((rows, width), BF16),
            jax.ShapeDtypeStruct((high, HALF), F32),
            jax.ShapeDtypeStruct((high, HALF), F32),
        ),
        in_specs=[vmem] * 5,
        out_specs=(vmem, vmem, vmem),
        scratch_shapes=scratch,
        compiler_params=pltpu.CompilerParams(
            vmem_limit_bytes=VMEM_LIMIT, collective_id=0, has_side_effects=True
        ),
    )(vectors, centroids, list_ids.reshape(1, rows), codes.T, rotation)
    table = jnp.concatenate([low, up], axis=1).reshape(owned, sub_width, K)
    return rotated, table.transpose(0, 2, 1).reshape(owned, K * sub_width)


def solution(mesh):
    in_specs = (
        P(("group", "within"), None),
        P(("group", "within"), None),
        P(("group", "within")),
        P(("group", "within"), None),
        P(),
    )
    out_specs = (P(("group", "within"), None), P("within", None))
    return jax.shard_map(
        per_device, mesh=mesh, in_specs=in_specs, out_specs=out_specs, check_vma=False
    )
```

```python
import functools

import jax
import jax.numpy as jnp
from jax import lax
from jax.experimental import pallas as pl
from jax.experimental.pallas import tpu as pltpu
from jax.sharding import PartitionSpec as P

K = 256
HALF = K // 2
HOT = HALF + 16
ALTS = 2
EPSILON = 1e-06
BATCH = 8
ROW_ORDER = (2, 3, 1, 0)
CUTS = ((0, 256), (256, 128))
MESH_ID = pl.DeviceIdType.MESH
NT = (((1,), (1,)), ((), ()))
VMEM_LIMIT = 60 * 1024 * 1024
F32, BF16 = jnp.float32, jnp.bfloat16


def dot_nt(left, right):
    return lax.dot_general(left, right, NT, preferred_element_type=F32)


def dot(left, right):
    return jnp.dot(left, right, preferred_element_type=F32)


def split_count(count):
    upper = jnp.floor(count * (1.0 / 256.0))
    return count - 256.0 * upper, upper


def whole_kernel(within, group, vec_ref, cen_ref, ids_ref, codes_s, rotation_ref,
                 out_ref, low_ref, up_ref, *scratch):
    (resid_s, rot_s, hot_s, urow_s, other_s, ucol_s, ccol_s, cnt_s, rec_s, rt_s, whole_s, low_s, gram_s,
     table_s, mate_t, send_t, plane_t, z_t, book_s,
     pair_ss, pair_rs, mate_ss, mate_rs, plane_ss, plane_rs, z_ss, z_rs,
     back_ss, back_rs, relay_ss, relay_rs) = scratch[:31]
    pieces_c = [scratch[31 + 6 * c : 37 + 6 * c] for c in range(len(CUTS))]
    rows, width = vec_ref.shape
    lists = cen_ref.shape[0]
    subspaces = codes_s.shape[0]
    chips = within // 2
    side = 4
    total_rows = rows * within * group
    owned = subspaces // within
    high = 8 * owned
    me_g = lax.axis_index("group")
    me_w = lax.axis_index("within")
    core = lax.rem(me_w, 2)
    chip = me_w // 2
    chip_y, chip_x = chip // side, lax.rem(chip, side)
    other_core = 1 - core
    mate = (me_g, me_w + 1 - 2 * core)
    device = me_g * within + me_w
    wide = width // 2
    tall = width // chips

    def chip_to(i):
        return lax.rem(chip_y + i // side, side) * side + lax.rem(chip_x + lax.rem(i, side), side)

    def chip_from(i):
        return lax.rem(chip_y + side - i // side, side) * side + lax.rem(
            chip_x + side - lax.rem(i, side), side
        )

    def plane_peer(i):
        return (me_g, 2 * chip_to(i) + core)

    def z_from(i):
        return lax.rem(me_g + group - lax.rem(3 * i, group), group)

    def z_peer(i):
        return (lax.rem(me_g + lax.rem(3 * i, group), group), me_w)

    def remote(src, dst, ss, rs, where):
        return pltpu.make_async_remote_copy(
            src_ref=src, dst_ref=dst, send_sem=ss, recv_sem=rs,
            device_id=where, device_id_type=MESH_ID,
        )

    def each(start, stop, body):
        def step(i, carry):
            body(i)
            return carry

        lax.fori_loop(start, stop, step, 0)

    def each_peer(body):
        each(2 * side, chips, body)
        each(side, 2 * side, body)
        each(1, side, body)

    def each_row(start, body):
        for dy in start:
            body(dy, side * lax.rem(chip_y + side - dy, side))

    barrier = pltpu.get_barrier_semaphore()
    pl.semaphore_signal(barrier, inc=1, device_id=mate, device_id_type=MESH_ID)
    each(1, chips, lambda i: pl.semaphore_signal(
        barrier, inc=1, device_id=plane_peer(i), device_id_type=MESH_ID))
    each(1, group, lambda i: pl.semaphore_signal(
        barrier, inc=1, device_id=z_peer(i), device_id_type=MESH_ID))

    local_list = jnp.broadcast_to(lax.rem(ids_ref[...], lists), (lists, rows))
    pick = jnp.where(lax.broadcasted_iota(jnp.int32, (lists, rows), 0) == local_list, 1.0, 0.0)
    pick = jnp.concatenate([pick, jnp.zeros((HALF - lists, rows), F32)], axis=0).T.astype(BF16)
    centre = cen_ref[...]
    pad = jnp.zeros((HALF - lists, width), F32)
    chosen = None
    for part in range(3):
        piece = centre.astype(BF16)
        centre = centre - piece.astype(F32)
        got = dot(pick, jnp.concatenate([piece.astype(F32), pad], axis=0).astype(BF16))
        chosen = got if chosen is None else chosen + got
    resid_s[...] = (vec_ref[...].astype(F32) - chosen).astype(BF16)

    urow_s[...] = jnp.zeros_like(urow_s)
    lane = lax.broadcasted_iota(jnp.int32, (1, HALF), 1)
    group_row = lax.broadcasted_iota(jnp.int32, (HALF, HALF), 0)
    lane_full = lax.broadcasted_iota(jnp.int32, (HALF, HALF), 1)

    def local_sums(alt):
        first = alt == 0
        levels = lax.broadcasted_iota(jnp.int32, (HOT, rows), 0)
        per_block = HALF // 8

        def block(b, counts):
            at = pl.multiple_of(b * HALF, HALF)
            right = rot_s[:, pl.ds(at, HALF)]
            if first:
                right = jnp.concatenate([right, jnp.ones((rows, HALF), BF16)], axis=1)
            total = jnp.zeros((HOT, HALF), F32)
            for start in range(0, per_block, BATCH):
                m0 = b * per_block + start
                if first:
                    for i in range(BATCH):
                        code = jnp.minimum(codes_s[pl.ds(m0 + i, 1), :], HALF)
                        hot_s[m0 + i] = jnp.where(levels == code, 1.0, 0.0).astype(BF16)
                hots = hot_s[pl.ds(m0, BATCH)].reshape(BATCH * HOT, rows)
                out = dot(hots, right)
                for i in range(BATCH):
                    at = 8 * (start + i)
                    here = (lane >= at) & (lane < at + 8)
                    mine = out[i * HOT : i * HOT + HOT]
                    total = jnp.where(here, mine[:, 0:HALF], total)
                    if first:
                        counts = jnp.where(lane == m0 + i, mine[:, HALF : 2 * HALF], counts)
            flipped = total[0:HALF].T
            for i in range(per_block):
                m = b * per_block + i
                w = m // owned
                spot = pl.multiple_of(8 * (m - w * owned), 8)
                table_s[alt, w // 2, lax.rem(w, 2), pl.ds(spot, 8), :] = flipped[8 * i : 8 * i + 8]
            urow_s[alt, pl.ds(b, 1), :] = total[HALF : HALF + 1]
            return counts

        counts = lax.fori_loop(0, width // HALF, block, jnp.zeros((HOT, HALF), F32))
        if first:
            urow_s[0, pl.ds(width // HALF, 1), :] = counts[HALF : HALF + 1]
            rec_c = counts[0:HALF].T
            upper = jnp.broadcast_to(urow_s[0].T[:, width // HALF : width // HALF + 1], (HALF, HALF))
            upper = jnp.where(lane_full == lax.rem(device + group_row, HALF), upper, 0.0)
            for w in range(within):
                for i in range(owned):
                    m = w * owned + i
                    table_s[0, w // 2, w % 2, high + i : high + i + 1, :] = rec_c[m : m + 1]
                    table_s[0, w // 2, w % 2, high + owned + i : high + owned + i + 1, :] = upper[
                        m : m + 1
                    ]
        else:
            columns = urow_s[alt].T
            for b in range(width // HALF):
                upper = jnp.broadcast_to(columns[:, b : b + 1], (HALF, HALF))
                spot = lax.rem(device + b * per_block + group_row // 8, HALF)
                upper = jnp.where(lane_full == spot, upper, 0.0)
                for i in range(per_block):
                    m = b * per_block + i
                    w = m // owned
                    at = high + 8 * (m % owned)
                    table_s[alt, w // 2, w % 2, at : at + 8, :] = upper[8 * i : 8 * i + 8]

    def reduce_sums(alt):
        size = high + 8 if alt == 0 else 2 * high
        sent = high + 16 if alt == 0 else 2 * high
        span = pl.ds(0, size)
        span16 = pl.ds(0, sent)

        def pack(part):
            if alt > 0:
                return part.astype(BF16)
            less, more = split_count(part[high : high + 8])
            return jnp.concatenate([part[0:high], less, more], axis=0).astype(BF16)

        def unpack(part):
            part = part.astype(F32)
            if alt > 0:
                return part
            count = part[high : high + 8] + 256.0 * part[high + 8 : high + 16]
            return jnp.concatenate([part[0:high], count], axis=0)

        give = remote(table_s.at[alt, :, other_core, span, :], mate_t.at[alt, :, span, :],
                      mate_ss.at[0, alt], mate_rs.at[0, alt], mate)
        give.start()
        swap = remote(urow_s.at[alt], other_s.at[alt], pair_ss.at[alt], pair_rs.at[alt],
                      (lax.rem(me_g + group // 2, group), me_w))
        swap.start()
        give.wait()

        def out1(i):
            return remote(send_t.at[alt, chip_to(i), span16, :],
                          plane_t.at[alt, i - 1, span16, :],
                          plane_ss.at[0, alt, i - 1], plane_rs.at[0, alt, i - 1], plane_peer(i))

        def go1(i):
            to = chip_to(i)
            send_t[alt, to, span16, :] = pack(
                table_s[alt, to, core, span, :] + mate_t[alt, to, span, :]
            )
            out1(i).start()

        each_peer(go1)
        flush()

        def take1(i, acc):
            out1(i).wait_recv()
            return acc + unpack(plane_t[alt, i - 1, span16, :])

        acc = table_s[alt, chip, core, span, :] + mate_t[alt, chip, span, :]
        z_t[alt, me_g, span16, :] = pack(lax.fori_loop(1, chips, take1, acc))

        def out2(i, slot):
            return remote(z_t.at[alt, slot, span16, :], z_t.at[alt, slot, span16, :],
                          z_ss.at[0, alt, i - 1], z_rs.at[0, alt, i - 1], z_peer(i))

        each(1, group, lambda i: out2(i, me_g).start())
        swap.wait()
        columns = (urow_s[alt] + other_s[alt]).T
        for b in range(width // HALF):
            ucol_s[b * HALF : b * HALF + HALF, :] = jnp.broadcast_to(
                columns[:, b : b + 1], (HALF, HALF)
            )
        if alt == 0:
            at = width // HALF
            ccol_s[...] = jnp.broadcast_to(columns[:, at : at + 1], (HALF, HALF)) + 1.0
        each(1, group, lambda i: out2(i, z_from(i)).wait_recv())
        total = unpack(z_t[alt, 0, span16, :])
        for g in range(1, group):
            total = total + unpack(z_t[alt, g, span16, :])
        if alt == 0:
            cnt_s[...] = total[high : high + 8] + 1.0
        counts = cnt_s[...]
        low = jnp.concatenate(
            [total[8 * i : 8 * i + 8] / counts[i : i + 1] for i in range(owned)], axis=0
        )
        book_s[alt, core, chip] = low.astype(BF16)

        def out3(i, slot):
            return remote(book_s.at[alt, core, slot], book_s.at[alt, core, slot],
                          back_ss.at[0, alt, i - 1], back_rs.at[0, alt, i - 1], plane_peer(i))

        def out4(half, slots, i):
            return remote(book_s.at[alt, half, slots], book_s.at[alt, half, slots],
                          relay_ss.at[0, alt, i], relay_rs.at[0, alt, i], mate)

        each_peer(lambda i: out3(i, chip).start())
        if alt == ALTS - 1:
            low_ref[...] = low
            up_ref[...] = jnp.concatenate(
                [total[high + 8 * i : high + 8 * i + 8] / counts[owned + i : owned + i + 1]
                 for i in range(owned)], axis=0,
            )

        def relay(dy, first_slot):
            each(max(1, side * dy), side * dy + side,
                 lambda i: out3(i, chip_from(i)).wait_recv())
            out4(core, pl.ds(first_slot, side), dy).start()

        each_row(ROW_ORDER, relay)
        each_row(ROW_ORDER, lambda dy, at: out4(other_core, pl.ds(at, side), dy).wait_recv())

        def gone(i):
            out1(i).wait_send()
            out3(i, chip).wait_send()

        def all_gone():
            each(1, chips, gone)
            each(1, group, lambda i: out2(i, me_g).wait_send())
            each_row(ROW_ORDER, lambda dy, at: out4(core, pl.ds(at, side), dy).wait_send())

        pending.append(all_gone)

    def rebuild(alt):
        def step(at, carry):
            table = jnp.concatenate([book_s[alt, 0, at], book_s[alt, 1, at]], axis=0).astype(F32)
            for pair in range(owned):
                pieces = []
                for sub in range(2):
                    local = 2 * pair + sub
                    m = at * (2 * owned) + local
                    words = table[8 * local : 8 * local + 8, :]
                    column = ucol_s[pl.ds(pl.multiple_of(8 * m, 8), 8), :] / ccol_s[pl.ds(m, 1), :]
                    row_pieces = []
                    code_row = codes_s[pl.ds(m, 1), :]
                    for part in range(rows // HALF):
                        code = jnp.broadcast_to(
                            code_row[:, HALF * part : HALF * part + HALF], (8, HALF)
                        )
                        low = jnp.take_along_axis(
                            words, jnp.bitwise_and(code, HALF - 1), axis=1,
                            mode="promise_in_bounds",
                        )
                        row_pieces.append(jnp.where(code >= HALF, column, low))
                    pieces.append(jnp.concatenate(row_pieces, axis=1))
                spot = pl.multiple_of(at * 16 * owned + 16 * pair, 16)
                rec_s[pl.ds(spot, 16), :] = jnp.concatenate(pieces, axis=0).astype(BF16)
            return carry

        lax.fori_loop(0, chips, step, 0)

    def reduce_cross(alt):
        gives = []
        for c, (start, size) in enumerate(CUTS):
            give_c, mate_c = pieces_c[c][0], pieces_c[c][1]
            at = pl.multiple_of(other_core * wide + start, HALF)
            give_c[alt, 0] = dot(rec_s[...], resid_s[:, pl.ds(at, size)]).astype(BF16).reshape(
                chips, tall, size
            )
            give = remote(give_c.at[alt, 0], mate_c.at[alt],
                          mate_ss.at[1 + c, alt], mate_rs.at[1 + c, alt], mate)
            give.start()
            gives.append(give)

        def out1(c, i):
            give_c, plane_c = pieces_c[c][0], pieces_c[c][2]
            return remote(give_c.at[alt, 1, chip_to(i)], plane_c.at[alt, i - 1],
                          plane_ss.at[1 + c, alt, i - 1], plane_rs.at[1 + c, alt, i - 1],
                          plane_peer(i))

        def out2(c, i, slot):
            z_c = pieces_c[c][3]
            return remote(z_c.at[alt, slot], z_c.at[alt, slot],
                          z_ss.at[1 + c, alt, i - 1], z_rs.at[1 + c, alt, i - 1], z_peer(i))

        def out3(c, i, slot):
            cross_s = pieces_c[c][4]
            return remote(cross_s.at[alt, core, slot], cross_s.at[alt, core, slot],
                          back_ss.at[1 + c, alt, i - 1], back_rs.at[1 + c, alt, i - 1],
                          plane_peer(i))

        def out4(c, half, slots, i):
            cross_s = pieces_c[c][4]
            return remote(cross_s.at[alt, half, slots], cross_s.at[alt, half, slots],
                          relay_ss.at[1 + c, alt, i], relay_rs.at[1 + c, alt, i], mate)

        for c, (start, size) in enumerate(CUTS):
            give_c, mate_c, own_c = pieces_c[c][0], pieces_c[c][1], pieces_c[c][5]
            at = pl.multiple_of(core * wide + start, HALF)
            own_c[...] = dot(rec_s[...], resid_s[:, pl.ds(at, size)]).reshape(chips, tall, size)
            gives[c].wait_recv()

            def go1(i):
                to = chip_to(i)
                give_c[alt, 1, to] = (own_c[to] + mate_c[alt, to].astype(F32)).astype(BF16)
                out1(c, i).start()

            each_peer(go1)
        flush()
        for c in range(len(CUTS)):
            mate_c, plane_c, z_c, own_c = (pieces_c[c][k] for k in (1, 2, 3, 5))

            def take1(i, acc):
                out1(c, i).wait_recv()
                return acc + plane_c[alt, i - 1].astype(F32)

            acc = own_c[chip] + mate_c[alt, chip].astype(F32)
            z_c[alt, me_g] = lax.fori_loop(1, chips, take1, acc).astype(BF16)
            each(1, group, lambda i: out2(c, i, me_g).start())
        for c in range(len(CUTS)):
            z_c, cross_s = pieces_c[c][3], pieces_c[c][4]
            each(1, group, lambda i: out2(c, i, z_from(i)).wait_recv())
            total = z_c[alt, 0].astype(F32)
            for g in range(1, group):
                total = total + z_c[alt, g].astype(F32)
            cross_s[alt, core, chip] = (total * (1.0 / total_rows)).astype(BF16)
            each_peer(lambda i: out3(c, i, chip).start())
        for c, (start, size) in enumerate(CUTS):
            cross_s = pieces_c[c][4]

            def relay(dy, first_slot):
                each(max(1, side * dy), side * dy + side,
                     lambda i: out3(c, i, chip_from(i)).wait_recv())
                out4(c, core, pl.ds(first_slot, side), dy).start()

            each_row(ROW_ORDER, relay)
            each_row(ROW_ORDER, lambda dy, at: out4(
                c, other_core, pl.ds(at, side), dy).wait_recv())
            for half in range(2):
                at = half * wide + start
                whole_s[:, at : at + size] = cross_s[alt, half].reshape(width, size)
            part = jnp.concatenate(
                [whole_s[:, half * wide + start : half * wide + start + size]
                 for half in range(2)], axis=1,
            )
            if c == 0:
                gram_s[...] = dot_nt(part, part)
            else:
                gram_s[...] += dot_nt(part, part)

        def all_gone():
            for c in range(len(CUTS)):

                def gone(i):
                    out1(c, i).wait_send()
                    out3(c, i, chip).wait_send()

                each(1, chips, gone)
                each(1, group, lambda i: out2(c, i, me_g).wait_send())
                each_row(ROW_ORDER, lambda dy, at: out4(
                    c, core, pl.ds(at, side), dy).wait_send())
                gives[c].wait_send()

        pending.append(all_gone)

    pending = []

    def flush():
        while pending:
            pending.pop(0)()

    def polar():
        blocks = [slice(at, at + width // 2) for at in range(0, width, width // 2)]
        square = jnp.zeros((8, width), F32)
        for block in blocks:
            gram = gram_s[block, :]
            square = square + jnp.sum((gram * gram).reshape(width // 16, 8, width), axis=0)
            low_s[block, :] = gram.astype(BF16)
        norm_square = jnp.sqrt(jnp.sum(square) + EPSILON)
        inv_square = 1.0 / norm_square
        inv_scale = jnp.sqrt(inv_square)
        near, far = 1.5 * inv_scale, 0.5 * inv_scale * inv_square
        for block in blocks:
            current = near * whole_s[block, :].astype(F32) - far * dot(low_s[block, :], whole_s[...])
            gram_s[block, :] = current
            rt_s[block, :] = current.astype(BF16)
        for block in blocks:
            low_s[block, :] = dot_nt(rt_s[block, :], rt_s[...]).astype(BF16)
        for block in blocks:
            whole_s[block, :] = (
                1.5 * gram_s[block, :] - 0.5 * dot(low_s[block, :], rt_s[...])
            ).astype(BF16)

    for alt in range(ALTS):
        if alt == 0:
            rot_s[...] = dot(resid_s[...], rotation_ref[...].astype(BF16)).astype(BF16)
        else:
            rot_s[...] = dot_nt(resid_s[...], whole_s[...]).astype(BF16)
        local_sums(alt)
        if alt == 0:
            pl.semaphore_wait(barrier, chips + group - 1)
        reduce_sums(alt)
        rebuild(alt)
        reduce_cross(alt)
        polar()
    out_ref[...] = dot_nt(resid_s[...], whole_s[...]).astype(BF16)
    flush()


def per_device(vectors, centroids, list_ids, codes, rotation):
    rows, width = vectors.shape
    subspaces = codes.shape[1]
    sub_width = width // subspaces
    within = lax.axis_size("within")
    group = lax.axis_size("group")
    owned = subspaces // within
    high = owned * sub_width
    chips = within // 2
    dma = pltpu.SemaphoreType.DMA
    vmem = pl.BlockSpec(memory_space=pltpu.VMEM)
    kinds = 1 + len(CUTS)
    scratch = [
        pltpu.VMEM((rows, width), BF16),
        pltpu.VMEM((rows, width), BF16),
        pltpu.VMEM((subspaces, HOT, rows), BF16),
        pltpu.VMEM((ALTS, 8, HALF), F32),
        pltpu.VMEM((ALTS, 8, HALF), F32),
        pltpu.VMEM((width, HALF), F32),
        pltpu.VMEM((HALF, HALF), F32),
        pltpu.VMEM((8, HALF), F32),
        pltpu.VMEM((width, rows), BF16),
        pltpu.VMEM((width, width), BF16),
        pltpu.VMEM((width, width), BF16),
        pltpu.VMEM((width, width), BF16),
        pltpu.VMEM((width, width), F32),
        pltpu.VMEM((ALTS, chips, 2, 2 * high, HALF), F32),
        pltpu.VMEM((ALTS, chips, 2 * high, HALF), F32),
        pltpu.VMEM((ALTS, chips, 2 * high, HALF), BF16),
        pltpu.VMEM((ALTS, chips - 1, 2 * high, HALF), BF16),
        pltpu.VMEM((ALTS, group, 2 * high, HALF), BF16),
        pltpu.VMEM((ALTS, 2, chips, high, HALF), BF16),
        dma((ALTS,)), dma((ALTS,)),
        dma((kinds, ALTS)), dma((kinds, ALTS)),
        dma((kinds, ALTS, chips - 1)), dma((kinds, ALTS, chips - 1)),
        dma((kinds, ALTS, group - 1)), dma((kinds, ALTS, group - 1)),
        dma((kinds, ALTS, chips - 1)), dma((kinds, ALTS, chips - 1)),
        dma((kinds, ALTS, chips)), dma((kinds, ALTS, chips)),
    ]
    for start, size in CUTS:
        block = (width // chips, size)
        scratch += [
            pltpu.VMEM((ALTS, 2, chips) + block, BF16),
            pltpu.VMEM((ALTS, chips) + block, BF16),
            pltpu.VMEM((ALTS, chips - 1) + block, BF16),
            pltpu.VMEM((ALTS, group) + block, BF16),
            pltpu.VMEM((ALTS, 2, chips) + block, BF16),
            pltpu.VMEM((chips,) + block, F32),
        ]
    rotated, low, up = pl.pallas_call(
        functools.partial(whole_kernel, within, group),
        out_shape=(
            jax.ShapeDtypeStruct((rows, width), BF16),
            jax.ShapeDtypeStruct((high, HALF), F32),
            jax.ShapeDtypeStruct((high, HALF), F32),
        ),
        in_specs=[vmem] * 5,
        out_specs=(vmem, vmem, vmem),
        scratch_shapes=scratch,
        compiler_params=pltpu.CompilerParams(
            vmem_limit_bytes=VMEM_LIMIT, collective_id=0, has_side_effects=True
        ),
    )(vectors, centroids, list_ids.reshape(1, rows), codes.T, rotation)
    table = jnp.concatenate([low, up], axis=1).reshape(owned, sub_width, K)
    return rotated, table.transpose(0, 2, 1).reshape(owned, K * sub_width)


def solution(mesh):
    in_specs = (
        P(("group", "within"), None),
        P(("group", "within"), None),
        P(("group", "within")),
        P(("group", "within"), None),
        P(),
    )
    out_specs = (P(("group", "within"), None), P("within", None))
    return jax.shard_map(
        per_device, mesh=mesh, in_specs=in_specs, out_specs=out_specs, check_vma=False
    )
```

```python
import functools

import jax
import jax.numpy as jnp
from jax import lax
from jax.experimental import pallas as pl
from jax.experimental.pallas import tpu as pltpu
from jax.sharding import PartitionSpec as P

K = 256
HALF = K // 2
HOT = HALF + 16
ALTS = 2
EPSILON = 1e-06
BATCH = 8
ROW_ORDER = (2, 3, 1, 0)
CUTS = ((0, 128), (128, 128), (256, 128))
MESH_ID = pl.DeviceIdType.MESH
NT = (((1,), (1,)), ((), ()))
VMEM_LIMIT = 48 * 1024 * 1024
F32, BF16 = jnp.float32, jnp.bfloat16


def dot_nt(left, right):
    return lax.dot_general(left, right, NT, preferred_element_type=F32)


def dot(left, right):
    return jnp.dot(left, right, preferred_element_type=F32)


def split_count(count):
    upper = jnp.floor(count * (1.0 / 256.0))
    return count - 256.0 * upper, upper


def whole_kernel(within, group, vec_ref, cen_ref, ids_ref, codes_s, rotation_ref,
                 resid_s, whole_s, words_ref, *scratch):
    (rot_s, hot_s, urow_s, other_s, ucol_s, ccol_s, cnt_s, rec_s, rt_s, low_s, gram_s,
     table_s, mate_t, send_t, plane_t, z_t, book_s,
     pair_ss, pair_rs, mate_ss, mate_rs, plane_ss, plane_rs, z_ss, z_rs,
     back_ss, back_rs, relay_ss, relay_rs) = scratch[:29]
    pieces_c = [scratch[29 + 6 * c : 35 + 6 * c] for c in range(len(CUTS))]
    rows, width = vec_ref.shape
    lists = cen_ref.shape[0]
    subspaces = codes_s.shape[0]
    chips = within // 2
    side = 4
    total_rows = rows * within * group
    owned = subspaces // within
    high = 8 * owned
    me_g = lax.axis_index("group")
    me_w = lax.axis_index("within")
    core = lax.rem(me_w, 2)
    chip = me_w // 2
    chip_y, chip_x = chip // side, lax.rem(chip, side)
    other_core = 1 - core
    mate = (me_g, me_w + 1 - 2 * core)
    device = me_g * within + me_w
    wide = width // 2
    tall = width // chips

    def chip_to(i):
        return lax.rem(chip_y + i // side, side) * side + lax.rem(chip_x + lax.rem(i, side), side)

    def chip_from(i):
        return lax.rem(chip_y + side - i // side, side) * side + lax.rem(
            chip_x + side - lax.rem(i, side), side
        )

    def plane_peer(i):
        return (me_g, 2 * chip_to(i) + core)

    def z_from(i):
        return lax.rem(me_g + group - lax.rem(3 * i, group), group)

    def z_peer(i):
        return (lax.rem(me_g + lax.rem(3 * i, group), group), me_w)

    def remote(src, dst, ss, rs, where):
        return pltpu.make_async_remote_copy(
            src_ref=src, dst_ref=dst, send_sem=ss, recv_sem=rs,
            device_id=where, device_id_type=MESH_ID,
        )

    def each(start, stop, body):
        def step(i, carry):
            body(i)
            return carry

        lax.fori_loop(start, stop, step, 0)

    def each_peer(body):
        each(2 * side, chips, body)
        each(side, 2 * side, body)
        each(1, side, body)

    def each_row(start, body):
        for dy in start:
            body(dy, side * lax.rem(chip_y + side - dy, side))

    barrier = pltpu.get_barrier_semaphore()
    pl.semaphore_signal(barrier, inc=1, device_id=mate, device_id_type=MESH_ID)
    each(1, chips, lambda i: pl.semaphore_signal(
        barrier, inc=1, device_id=plane_peer(i), device_id_type=MESH_ID))
    each(1, group, lambda i: pl.semaphore_signal(
        barrier, inc=1, device_id=z_peer(i), device_id_type=MESH_ID))

    local_list = jnp.broadcast_to(lax.rem(ids_ref[...], lists), (lists, rows))
    pick = jnp.where(lax.broadcasted_iota(jnp.int32, (lists, rows), 0) == local_list, 1.0, 0.0)
    pick = jnp.concatenate([pick, pick, pick, jnp.zeros((lists, rows), F32)], axis=0)
    pick = pick.T.astype(BF16)
    centre = cen_ref[...]
    parts = []
    for part in range(3):
        parts.append(centre.astype(BF16).astype(F32))
        centre = centre - parts[-1]
    parts = jnp.concatenate(parts + [jnp.zeros((lists, width), F32)], axis=0).astype(BF16)
    resid_s[...] = (vec_ref[...].astype(F32) - dot(pick, parts)).astype(BF16)

    urow_s[...] = jnp.zeros_like(urow_s)
    lane = lax.broadcasted_iota(jnp.int32, (1, HALF), 1)
    group_row = lax.broadcasted_iota(jnp.int32, (HALF, HALF), 0)
    lane_full = lax.broadcasted_iota(jnp.int32, (HALF, HALF), 1)

    def local_sums(alt):
        first = alt == 0
        levels = lax.broadcasted_iota(jnp.int32, (HOT, rows), 0).astype(F32).astype(BF16)
        per_block = HALF // 8

        def block(b, counts):
            at = pl.multiple_of(b * HALF, HALF)
            right = rot_s[:, pl.ds(at, HALF)]
            if first:
                right = jnp.concatenate([right, jnp.ones((rows, HALF), BF16)], axis=1)
            total = jnp.zeros((HOT, HALF), F32)
            for start in range(0, per_block, BATCH):
                m0 = b * per_block + start
                if first:
                    for i in range(BATCH):
                        code = jnp.minimum(codes_s[pl.ds(m0 + i, 1), :], HALF).astype(F32).astype(BF16)
                        hot_s[m0 + i] = jnp.where(levels == code, jnp.bfloat16(1), jnp.bfloat16(0))
                hots = hot_s[pl.ds(m0, BATCH)].reshape(BATCH * HOT, rows)
                out = dot(hots, right)
                for i in range(BATCH):
                    at = 8 * (start + i)
                    here = (lane >= at) & (lane < at + 8)
                    mine = out[i * HOT : i * HOT + HOT]
                    total = jnp.where(here, mine[:, 0:HALF], total)
                    if first:
                        counts = jnp.where(lane == m0 + i, mine[:, HALF : 2 * HALF], counts)
            flipped = total[0:HALF].T
            for i in range(per_block):
                m = b * per_block + i
                w = m // owned
                spot = pl.multiple_of(8 * (m - w * owned), 8)
                table_s[alt, w // 2, lax.rem(w, 2), pl.ds(spot, 8), :] = flipped[8 * i : 8 * i + 8]
            urow_s[alt, pl.ds(b, 1), :] = total[HALF : HALF + 1]
            return counts

        counts = lax.fori_loop(0, width // HALF, block, jnp.zeros((HOT, HALF), F32))
        if first:
            urow_s[0, pl.ds(width // HALF, 1), :] = counts[HALF : HALF + 1]
            rec_c = counts[0:HALF].T
            upper = jnp.broadcast_to(urow_s[0].T[:, width // HALF : width // HALF + 1], (HALF, HALF))
            upper = jnp.where(lane_full == lax.rem(device + group_row, HALF), upper, 0.0)
            for w in range(within):
                for i in range(owned):
                    m = w * owned + i
                    table_s[0, w // 2, w % 2, high + i : high + i + 1, :] = rec_c[m : m + 1]
                    table_s[0, w // 2, w % 2, high + owned + i : high + owned + i + 1, :] = upper[
                        m : m + 1
                    ]
        else:
            columns = urow_s[alt].T
            for b in range(width // HALF):
                upper = jnp.broadcast_to(columns[:, b : b + 1], (HALF, HALF))
                spot = lax.rem(device + b * per_block + group_row // 8, HALF)
                upper = jnp.where(lane_full == spot, upper, 0.0)
                for i in range(per_block):
                    m = b * per_block + i
                    w = m // owned
                    at = high + 8 * (m % owned)
                    table_s[alt, w // 2, w % 2, at : at + 8, :] = upper[8 * i : 8 * i + 8]

    def reduce_sums(alt):
        size = high + 8 if alt == 0 else 2 * high
        sent = high + 16 if alt == 0 else 2 * high
        span = pl.ds(0, size)
        span16 = pl.ds(0, sent)

        def pack(part):
            if alt > 0:
                return part.astype(BF16)
            less, more = split_count(part[high : high + 8])
            return jnp.concatenate([part[0:high], less, more], axis=0).astype(BF16)

        def unpack(part):
            part = part.astype(F32)
            if alt > 0:
                return part
            count = part[high : high + 8] + 256.0 * part[high + 8 : high + 16]
            return jnp.concatenate([part[0:high], count], axis=0)

        give = remote(table_s.at[alt, :, other_core, span, :], mate_t.at[alt, :, span, :],
                      mate_ss.at[0, alt], mate_rs.at[0, alt], mate)
        give.start()
        swap = remote(urow_s.at[alt], other_s.at[alt], pair_ss.at[alt], pair_rs.at[alt],
                      (lax.rem(me_g + group // 2, group), me_w))
        swap.start()
        give.wait()

        def out1(i):
            return remote(send_t.at[alt, chip_to(i), span16, :],
                          plane_t.at[alt, i - 1, span16, :],
                          plane_ss.at[0, alt, i - 1], plane_rs.at[0, alt, i - 1], plane_peer(i))

        def go1(i):
            to = chip_to(i)
            send_t[alt, to, span16, :] = pack(
                table_s[alt, to, core, span, :] + mate_t[alt, to, span, :]
            )
            out1(i).start()

        each_peer(go1)
        flush()

        def take1(i, acc):
            out1(i).wait_recv()
            return acc + unpack(plane_t[alt, i - 1, span16, :])

        acc = table_s[alt, chip, core, span, :] + mate_t[alt, chip, span, :]
        z_t[alt, me_g, span16, :] = pack(lax.fori_loop(1, chips, take1, acc))

        def out2(i, slot):
            return remote(z_t.at[alt, slot, span16, :], z_t.at[alt, slot, span16, :],
                          z_ss.at[0, alt, i - 1], z_rs.at[0, alt, i - 1], z_peer(i))

        each(1, group, lambda i: out2(i, me_g).start())
        swap.wait()
        columns = (urow_s[alt] + other_s[alt]).T
        for b in range(width // HALF):
            ucol_s[b * HALF : b * HALF + HALF, :] = jnp.broadcast_to(
                columns[:, b : b + 1], (HALF, HALF)
            )
        if alt == 0:
            at = width // HALF
            ccol_s[...] = jnp.broadcast_to(columns[:, at : at + 1], (HALF, HALF)) + 1.0
        each(1, group, lambda i: out2(i, z_from(i)).wait_recv())
        total = unpack(z_t[alt, 0, span16, :])
        for g in range(1, group):
            total = total + unpack(z_t[alt, g, span16, :])
        if alt == 0:
            cnt_s[...] = total[high : high + 8] + 1.0
        counts = cnt_s[...]
        low = jnp.concatenate(
            [total[8 * i : 8 * i + 8] / counts[i : i + 1] for i in range(owned)], axis=0
        )
        book_s[alt, core, chip] = low.astype(BF16)

        def out3(i, slot):
            return remote(book_s.at[alt, core, slot], book_s.at[alt, core, slot],
                          back_ss.at[0, alt, i - 1], back_rs.at[0, alt, i - 1], plane_peer(i))

        def out4(half, slots, i):
            return remote(book_s.at[alt, half, slots], book_s.at[alt, half, slots],
                          relay_ss.at[0, alt, i], relay_rs.at[0, alt, i], mate)

        each_peer(lambda i: out3(i, chip).start())
        if alt == ALTS - 1:
            up = jnp.concatenate(
                [total[high + 8 * i : high + 8 * i + 8] / counts[owned + i : owned + i + 1]
                 for i in range(owned)], axis=0,
            )
            lanes = lax.broadcasted_iota(jnp.int32, (8, HALF), 1)
            diagonal = lax.broadcasted_iota(jnp.int32, (8, HALF), 0) == lax.rem(lanes, 8)
            for i in range(owned):
                for q in range(K // 16):
                    half = low if q < K // 32 else up
                    picked = jnp.take_along_axis(
                        half[8 * i : 8 * i + 8], lanes // 8 + 16 * (q % 8), axis=1,
                        mode="promise_in_bounds",
                    )
                    words_ref[i : i + 1, HALF * q : HALF * q + HALF] = jnp.sum(
                        jnp.where(diagonal, picked, 0.0), axis=0, keepdims=True
                    )

        def relay(dy, first_slot):
            each(max(1, side * dy), side * dy + side,
                 lambda i: out3(i, chip_from(i)).wait_recv())
            out4(core, pl.ds(first_slot, side), dy).start()

        each_row(ROW_ORDER, relay)
        each_row(ROW_ORDER, lambda dy, at: out4(other_core, pl.ds(at, side), dy).wait_recv())

        def gone(i):
            out1(i).wait_send()
            out3(i, chip).wait_send()

        def all_gone():
            each(1, chips, gone)
            each(1, group, lambda i: out2(i, me_g).wait_send())
            each_row(ROW_ORDER, lambda dy, at: out4(core, pl.ds(at, side), dy).wait_send())

        pending.append(all_gone)

    def rebuild(alt):
        def step(at, carry):
            table = jnp.concatenate([book_s[alt, 0, at], book_s[alt, 1, at]], axis=0).astype(F32)
            for pair in range(owned):
                pieces = []
                for sub in range(2):
                    local = 2 * pair + sub
                    m = at * (2 * owned) + local
                    words = table[8 * local : 8 * local + 8, :]
                    column = ucol_s[pl.ds(pl.multiple_of(8 * m, 8), 8), :] / ccol_s[pl.ds(m, 1), :]
                    row_pieces = []
                    code_row = codes_s[pl.ds(m, 1), :]
                    for part in range(rows // HALF):
                        code = jnp.broadcast_to(
                            code_row[:, HALF * part : HALF * part + HALF], (8, HALF)
                        )
                        low = jnp.take_along_axis(
                            words, jnp.bitwise_and(code, HALF - 1), axis=1,
                            mode="promise_in_bounds",
                        )
                        row_pieces.append(jnp.where(code >= HALF, column, low))
                    pieces.append(jnp.concatenate(row_pieces, axis=1))
                spot = pl.multiple_of(at * 16 * owned + 16 * pair, 16)
                rec_s[pl.ds(spot, 16), :] = jnp.concatenate(pieces, axis=0).astype(BF16)
            return carry

        lax.fori_loop(0, chips, step, 0)

    def reduce_cross(alt):
        gives = []
        for c, (start, size) in enumerate(CUTS):
            give_c, mate_c = pieces_c[c][0], pieces_c[c][1]
            at = pl.multiple_of(other_core * wide + start, HALF)
            give_c[alt, 0] = dot(rec_s[...], resid_s[:, pl.ds(at, size)]).astype(BF16).reshape(
                chips, tall, size
            )
            give = remote(give_c.at[alt, 0], mate_c.at[alt],
                          mate_ss.at[1 + c, alt], mate_rs.at[1 + c, alt], mate)
            give.start()
            gives.append(give)

        def out1(c, i):
            give_c, plane_c = pieces_c[c][0], pieces_c[c][2]
            return remote(give_c.at[alt, 1, chip_to(i)], plane_c.at[alt, i - 1],
                          plane_ss.at[1 + c, alt, i - 1], plane_rs.at[1 + c, alt, i - 1],
                          plane_peer(i))

        def out2(c, i, slot):
            z_c = pieces_c[c][3]
            return remote(z_c.at[alt, slot], z_c.at[alt, slot],
                          z_ss.at[1 + c, alt, i - 1], z_rs.at[1 + c, alt, i - 1], z_peer(i))

        def out3(c, i, slot):
            cross_s = pieces_c[c][4]
            return remote(cross_s.at[alt, core, slot], cross_s.at[alt, core, slot],
                          back_ss.at[1 + c, alt, i - 1], back_rs.at[1 + c, alt, i - 1],
                          plane_peer(i))

        def out4(c, half, slots, i):
            cross_s = pieces_c[c][4]
            return remote(cross_s.at[alt, half, slots], cross_s.at[alt, half, slots],
                          relay_ss.at[1 + c, alt, i], relay_rs.at[1 + c, alt, i], mate)

        for c, (start, size) in enumerate(CUTS):
            give_c, mate_c, own_c = pieces_c[c][0], pieces_c[c][1], pieces_c[c][5]
            at = pl.multiple_of(core * wide + start, HALF)
            own_c[...] = dot(rec_s[...], resid_s[:, pl.ds(at, size)]).reshape(chips, tall, size)
            gives[c].wait_recv()

            def go1(i):
                to = chip_to(i)
                give_c[alt, 1, to] = (own_c[to] + mate_c[alt, to].astype(F32)).astype(BF16)
                out1(c, i).start()

            each_peer(go1)
        flush()
        for c in range(len(CUTS)):
            mate_c, plane_c, z_c, own_c = (pieces_c[c][k] for k in (1, 2, 3, 5))

            def take1(i, acc):
                out1(c, i).wait_recv()
                return acc + plane_c[alt, i - 1].astype(F32)

            acc = own_c[chip] + mate_c[alt, chip].astype(F32)
            z_c[alt, me_g] = lax.fori_loop(1, chips, take1, acc).astype(BF16)
            each(1, group, lambda i: out2(c, i, me_g).start())
        for c in range(len(CUTS)):
            z_c, cross_s = pieces_c[c][3], pieces_c[c][4]
            each(1, group, lambda i: out2(c, i, z_from(i)).wait_recv())
            total = z_c[alt, 0].astype(F32)
            for g in range(1, group):
                total = total + z_c[alt, g].astype(F32)
            cross_s[alt, core, chip] = (total * (1.0 / total_rows)).astype(BF16)
            each_peer(lambda i: out3(c, i, chip).start())
        for c, (start, size) in enumerate(CUTS):
            cross_s = pieces_c[c][4]

            def relay(dy, first_slot):
                each(max(1, side * dy), side * dy + side,
                     lambda i: out3(c, i, chip_from(i)).wait_recv())
                out4(c, core, pl.ds(first_slot, side), dy).start()

            each_row(ROW_ORDER, relay)
            each_row(ROW_ORDER, lambda dy, at: out4(
                c, other_core, pl.ds(at, side), dy).wait_recv())
            for half in range(2):
                at = half * wide + start
                whole_s[:, at : at + size] = cross_s[alt, half].reshape(width, size)
            part = jnp.concatenate(
                [whole_s[:, half * wide + start : half * wide + start + size]
                 for half in range(2)], axis=1,
            )
            if c == 0:
                gram_s[...] = dot_nt(part, part)
            else:
                gram_s[...] += dot_nt(part, part)

        def all_gone():
            for c in range(len(CUTS)):

                def gone(i):
                    out1(c, i).wait_send()
                    out3(c, i, chip).wait_send()

                each(1, chips, gone)
                each(1, group, lambda i: out2(c, i, me_g).wait_send())
                each_row(ROW_ORDER, lambda dy, at: out4(
                    c, core, pl.ds(at, side), dy).wait_send())
                gives[c].wait_send()

        pending.append(all_gone)

    pending = []

    def flush():
        while pending:
            pending.pop(0)()

    def polar():
        blocks = [slice(at, at + width // 2) for at in range(0, width, width // 2)]
        square = jnp.zeros((8, width), F32)
        for block in blocks:
            gram = gram_s[block, :]
            square = square + jnp.sum((gram * gram).reshape(width // 16, 8, width), axis=0)
            low_s[block, :] = gram.astype(BF16)
        norm_square = jnp.sqrt(jnp.sum(square) + EPSILON)
        inv_square = 1.0 / norm_square
        inv_scale = jnp.sqrt(inv_square)
        near, far = 1.5 * inv_scale, 0.5 * inv_scale * inv_square
        for block in blocks:
            current = near * whole_s[block, :].astype(F32) - far * dot(low_s[block, :], whole_s[...])
            gram_s[block, :] = current
            rt_s[block, :] = current.astype(BF16)
        for block in blocks:
            low_s[block, :] = dot_nt(rt_s[block, :], rt_s[...]).astype(BF16)
        for block in blocks:
            whole_s[block, :] = (
                1.5 * gram_s[block, :] - 0.5 * dot(low_s[block, :], rt_s[...])
            ).astype(BF16)

    for alt in range(ALTS):
        if alt == 0:
            rot_s[...] = dot(resid_s[...], rotation_ref[...].astype(BF16)).astype(BF16)
        else:
            rot_s[...] = dot_nt(resid_s[...], whole_s[...]).astype(BF16)
        local_sums(alt)
        if alt == 0:
            pl.semaphore_wait(barrier, chips + group - 1)
        reduce_sums(alt)
        rebuild(alt)
        reduce_cross(alt)
        polar()
    flush()


def per_device(vectors, centroids, list_ids, codes, rotation):
    rows, width = vectors.shape
    subspaces = codes.shape[1]
    sub_width = width // subspaces
    within = lax.axis_size("within")
    group = lax.axis_size("group")
    owned = subspaces // within
    high = owned * sub_width
    chips = within // 2
    dma = pltpu.SemaphoreType.DMA
    vmem = pl.BlockSpec(memory_space=pltpu.VMEM)
    kinds = 1 + len(CUTS)
    scratch = [
        pltpu.VMEM((rows, width), BF16),
        pltpu.VMEM((subspaces, HOT, rows), BF16),
        pltpu.VMEM((ALTS, 8, HALF), F32),
        pltpu.VMEM((ALTS, 8, HALF), F32),
        pltpu.VMEM((width, HALF), F32),
        pltpu.VMEM((HALF, HALF), F32),
        pltpu.VMEM((8, HALF), F32),
        pltpu.VMEM((width, rows), BF16),
        pltpu.VMEM((width, width), BF16),
        pltpu.VMEM((width, width), BF16),
        pltpu.VMEM((width, width), F32),
        pltpu.VMEM((ALTS, chips, 2, 2 * high, HALF), F32),
        pltpu.VMEM((ALTS, chips, 2 * high, HALF), F32),
        pltpu.VMEM((ALTS, chips, 2 * high, HALF), BF16),
        pltpu.VMEM((ALTS, chips - 1, 2 * high, HALF), BF16),
        pltpu.VMEM((ALTS, group, 2 * high, HALF), BF16),
        pltpu.VMEM((ALTS, 2, chips, high, HALF), BF16),
        dma((ALTS,)), dma((ALTS,)),
        dma((kinds, ALTS)), dma((kinds, ALTS)),
        dma((kinds, ALTS, chips - 1)), dma((kinds, ALTS, chips - 1)),
        dma((kinds, ALTS, group - 1)), dma((kinds, ALTS, group - 1)),
        dma((kinds, ALTS, chips - 1)), dma((kinds, ALTS, chips - 1)),
        dma((kinds, ALTS, chips)), dma((kinds, ALTS, chips)),
    ]
    for start, size in CUTS:
        block = (width // chips, size)
        scratch += [
            pltpu.VMEM((ALTS, 2, chips) + block, BF16),
            pltpu.VMEM((ALTS, chips) + block, BF16),
            pltpu.VMEM((ALTS, chips - 1) + block, BF16),
            pltpu.VMEM((ALTS, group) + block, BF16),
            pltpu.VMEM((ALTS, 2, chips) + block, BF16),
            pltpu.VMEM((chips,) + block, F32),
        ]
    resid, turned, words = pl.pallas_call(
        functools.partial(whole_kernel, within, group),
        out_shape=(
            jax.ShapeDtypeStruct((rows, width), BF16),
            jax.ShapeDtypeStruct((width, width), BF16),
            jax.ShapeDtypeStruct((owned, sub_width * K), F32),
        ),
        in_specs=[vmem] * 5,
        out_specs=(vmem, vmem, vmem),
        scratch_shapes=scratch,
        compiler_params=pltpu.CompilerParams(
            vmem_limit_bytes=VMEM_LIMIT, collective_id=0, has_side_effects=True
        ),
    )(vectors, centroids, list_ids.reshape(1, rows), codes.T, rotation)
    return dot_nt(resid, turned).astype(BF16), words


def solution(mesh):
    in_specs = (
        P(("group", "within"), None),
        P(("group", "within"), None),
        P(("group", "within")),
        P(("group", "within"), None),
        P(),
    )
    out_specs = (P(("group", "within"), None), P("within", None))
    return jax.shard_map(
        per_device, mesh=mesh, in_specs=in_specs, out_specs=out_specs, check_vma=False
    )
```

```python
import functools

import jax
import jax.numpy as jnp
from jax import lax
from jax.experimental import pallas as pl
from jax.experimental.pallas import tpu as pltpu
from jax.sharding import PartitionSpec as P

K = 256
HALF = K // 2
HOT = HALF + 16
ALTS = 2
EPSILON = 1e-06
BATCH = 8
ROW_ORDER = (2, 3, 1, 0)
CUTS = ((0, 128), (128, 128), (256, 128))
MESH_ID = pl.DeviceIdType.MESH
NT = (((1,), (1,)), ((), ()))
VMEM_LIMIT = 48 * 1024 * 1024
F32, BF16 = jnp.float32, jnp.bfloat16


def dot_nt(left, right):
    return lax.dot_general(left, right, NT, preferred_element_type=F32)


def dot(left, right):
    return jnp.dot(left, right, preferred_element_type=F32)


def split_count(count):
    upper = jnp.floor(count * (1.0 / 256.0))
    return count - 256.0 * upper, upper


def whole_kernel(within, group, vec_ref, cen_ref, ids_ref, codes_ref, rotation_ref,
                 resid_s, whole_s, words_ref, *scratch):
    (cen_s, ids_s, codes_s, load_sem, rot_s, hot_s, urow_s, other_s, ucol_s, ccol_s, cnt_s, rec_s, rt_s, low_s, gram_s,
     table_s, mate_t, send_t, plane_t, z_t, book_s,
     pair_ss, pair_rs, mate_ss, mate_rs, plane_ss, plane_rs, z_ss, z_rs,
     back_ss, back_rs, relay_ss, relay_rs) = scratch[:33]
    pieces_c = [scratch[33 + 6 * c : 39 + 6 * c] for c in range(len(CUTS))]
    rows, width = vec_ref.shape
    lists = cen_ref.shape[0]
    subspaces = codes_s.shape[0]
    chips = within // 2
    side = 4
    total_rows = rows * within * group
    owned = subspaces // within
    high = 8 * owned
    me_g = lax.axis_index("group")
    me_w = lax.axis_index("within")
    core = lax.rem(me_w, 2)
    chip = me_w // 2
    chip_y, chip_x = chip // side, lax.rem(chip, side)
    other_core = 1 - core
    mate = (me_g, me_w + 1 - 2 * core)
    device = me_g * within + me_w
    wide = width // 2
    tall = width // chips

    def chip_to(i):
        return lax.rem(chip_y + i // side, side) * side + lax.rem(chip_x + lax.rem(i, side), side)

    def chip_from(i):
        return lax.rem(chip_y + side - i // side, side) * side + lax.rem(
            chip_x + side - lax.rem(i, side), side
        )

    def plane_peer(i):
        return (me_g, 2 * chip_to(i) + core)

    def z_from(i):
        return lax.rem(me_g + group - lax.rem(3 * i, group), group)

    def z_peer(i):
        return (lax.rem(me_g + lax.rem(3 * i, group), group), me_w)

    def remote(src, dst, ss, rs, where):
        return pltpu.make_async_remote_copy(
            src_ref=src, dst_ref=dst, send_sem=ss, recv_sem=rs,
            device_id=where, device_id_type=MESH_ID,
        )

    def each(start, stop, body):
        def step(i, carry):
            body(i)
            return carry

        lax.fori_loop(start, stop, step, 0)

    def each_peer(body):
        each(2 * side, chips, body)
        each(side, 2 * side, body)
        each(1, side, body)

    def each_row(start, body):
        for dy in start:
            body(dy, side * lax.rem(chip_y + side - dy, side))

    loads = [
        pltpu.make_async_copy(src, dst, load_sem.at[k])
        for k, (src, dst) in enumerate((
            (ids_ref, ids_s), (cen_ref, cen_s), (vec_ref, rot_s),
            (codes_ref, codes_s), (rotation_ref, gram_s),
        ))
    ]
    for load in loads:
        load.start()

    barrier = pltpu.get_barrier_semaphore()
    pl.semaphore_signal(barrier, inc=1, device_id=mate, device_id_type=MESH_ID)
    each(1, chips, lambda i: pl.semaphore_signal(
        barrier, inc=1, device_id=plane_peer(i), device_id_type=MESH_ID))
    each(1, group, lambda i: pl.semaphore_signal(
        barrier, inc=1, device_id=z_peer(i), device_id_type=MESH_ID))

    for load in loads[:3]:
        load.wait()
    local_list = jnp.broadcast_to(lax.rem(ids_s[...], lists), (lists, rows))
    pick = jnp.where(lax.broadcasted_iota(jnp.int32, (lists, rows), 0) == local_list, 1.0, 0.0)
    pick = jnp.concatenate([pick, pick, pick, jnp.zeros((lists, rows), F32)], axis=0)
    pick = pick.T.astype(BF16)
    centre = cen_s[...]
    parts = []
    for part in range(3):
        parts.append(centre.astype(BF16).astype(F32))
        centre = centre - parts[-1]
    parts = jnp.concatenate(parts + [jnp.zeros((lists, width), F32)], axis=0).astype(BF16)
    resid_s[...] = (rot_s[...].astype(F32) - dot(pick, parts)).astype(BF16)

    urow_s[...] = jnp.zeros_like(urow_s)
    lane = lax.broadcasted_iota(jnp.int32, (1, HALF), 1)
    group_row = lax.broadcasted_iota(jnp.int32, (HALF, HALF), 0)
    lane_full = lax.broadcasted_iota(jnp.int32, (HALF, HALF), 1)

    def local_sums(alt):
        first = alt == 0
        levels = lax.broadcasted_iota(jnp.int32, (HOT, rows), 0).astype(F32).astype(BF16)
        per_block = HALF // 8

        def block(b, counts):
            at = pl.multiple_of(b * HALF, HALF)
            right = rot_s[:, pl.ds(at, HALF)]
            if first:
                right = jnp.concatenate([right, jnp.ones((rows, HALF), BF16)], axis=1)
            total = jnp.zeros((HOT, HALF), F32)
            for start in range(0, per_block, BATCH):
                m0 = b * per_block + start
                if first:
                    for i in range(BATCH):
                        code = jnp.minimum(codes_s[pl.ds(m0 + i, 1), :], HALF).astype(F32).astype(BF16)
                        hot_s[m0 + i] = jnp.where(levels == code, jnp.bfloat16(1), jnp.bfloat16(0))
                hots = hot_s[pl.ds(m0, BATCH)].reshape(BATCH * HOT, rows)
                out = dot(hots, right)
                for i in range(BATCH):
                    at = 8 * (start + i)
                    here = (lane >= at) & (lane < at + 8)
                    mine = out[i * HOT : i * HOT + HOT]
                    total = jnp.where(here, mine[:, 0:HALF], total)
                    if first:
                        counts = jnp.where(lane == m0 + i, mine[:, HALF : 2 * HALF], counts)
            flipped = total[0:HALF].T
            for i in range(per_block):
                m = b * per_block + i
                w = m // owned
                spot = pl.multiple_of(8 * (m - w * owned), 8)
                table_s[alt, w // 2, lax.rem(w, 2), pl.ds(spot, 8), :] = flipped[8 * i : 8 * i + 8]
            urow_s[alt, pl.ds(b, 1), :] = total[HALF : HALF + 1]
            return counts

        counts = lax.fori_loop(0, width // HALF, block, jnp.zeros((HOT, HALF), F32))
        if first:
            urow_s[0, pl.ds(width // HALF, 1), :] = counts[HALF : HALF + 1]
            rec_c = counts[0:HALF].T
            upper = jnp.broadcast_to(urow_s[0].T[:, width // HALF : width // HALF + 1], (HALF, HALF))
            upper = jnp.where(lane_full == lax.rem(device + group_row, HALF), upper, 0.0)
            for w in range(within):
                for i in range(owned):
                    m = w * owned + i
                    table_s[0, w // 2, w % 2, high + i : high + i + 1, :] = rec_c[m : m + 1]
                    table_s[0, w // 2, w % 2, high + owned + i : high + owned + i + 1, :] = upper[
                        m : m + 1
                    ]
        else:
            columns = urow_s[alt].T
            for b in range(width // HALF):
                upper = jnp.broadcast_to(columns[:, b : b + 1], (HALF, HALF))
                spot = lax.rem(device + b * per_block + group_row // 8, HALF)
                upper = jnp.where(lane_full == spot, upper, 0.0)
                for i in range(per_block):
                    m = b * per_block + i
                    w = m // owned
                    at = high + 8 * (m % owned)
                    table_s[alt, w // 2, w % 2, at : at + 8, :] = upper[8 * i : 8 * i + 8]

    def reduce_sums(alt):
        size = high + 8 if alt == 0 else 2 * high
        sent = high + 16 if alt == 0 else 2 * high
        span = pl.ds(0, size)
        span16 = pl.ds(0, sent)

        def pack(part):
            if alt > 0:
                return part.astype(BF16)
            less, more = split_count(part[high : high + 8])
            return jnp.concatenate([part[0:high], less, more], axis=0).astype(BF16)

        def unpack(part):
            part = part.astype(F32)
            if alt > 0:
                return part
            count = part[high : high + 8] + 256.0 * part[high + 8 : high + 16]
            return jnp.concatenate([part[0:high], count], axis=0)

        give = remote(table_s.at[alt, :, other_core, span, :], mate_t.at[alt, :, span, :],
                      mate_ss.at[0, alt], mate_rs.at[0, alt], mate)
        give.start()
        swap = remote(urow_s.at[alt], other_s.at[alt], pair_ss.at[alt], pair_rs.at[alt],
                      (lax.rem(me_g + group // 2, group), me_w))
        swap.start()
        give.wait()

        def out1(i):
            return remote(send_t.at[alt, chip_to(i), span16, :],
                          plane_t.at[alt, i - 1, span16, :],
                          plane_ss.at[0, alt, i - 1], plane_rs.at[0, alt, i - 1], plane_peer(i))

        def go1(i):
            to = chip_to(i)
            send_t[alt, to, span16, :] = pack(
                table_s[alt, to, core, span, :] + mate_t[alt, to, span, :]
            )
            out1(i).start()

        each_peer(go1)
        flush()

        def take1(i, acc):
            out1(i).wait_recv()
            return acc + unpack(plane_t[alt, i - 1, span16, :])

        acc = table_s[alt, chip, core, span, :] + mate_t[alt, chip, span, :]
        z_t[alt, me_g, span16, :] = pack(lax.fori_loop(1, chips, take1, acc))

        def out2(i, slot):
            return remote(z_t.at[alt, slot, span16, :], z_t.at[alt, slot, span16, :],
                          z_ss.at[0, alt, i - 1], z_rs.at[0, alt, i - 1], z_peer(i))

        each(1, group, lambda i: out2(i, me_g).start())
        swap.wait()
        columns = (urow_s[alt] + other_s[alt]).T
        for b in range(width // HALF):
            ucol_s[b * HALF : b * HALF + HALF, :] = jnp.broadcast_to(
                columns[:, b : b + 1], (HALF, HALF)
            )
        if alt == 0:
            at = width // HALF
            ccol_s[...] = jnp.broadcast_to(columns[:, at : at + 1], (HALF, HALF)) + 1.0
        each(1, group, lambda i: out2(i, z_from(i)).wait_recv())
        total = unpack(z_t[alt, 0, span16, :])
        for g in range(1, group):
            total = total + unpack(z_t[alt, g, span16, :])
        if alt == 0:
            cnt_s[...] = total[high : high + 8] + 1.0
        counts = cnt_s[...]
        low = jnp.concatenate(
            [total[8 * i : 8 * i + 8] / counts[i : i + 1] for i in range(owned)], axis=0
        )
        book_s[alt, core, chip] = low.astype(BF16)

        def out3(i, slot):
            return remote(book_s.at[alt, core, slot], book_s.at[alt, core, slot],
                          back_ss.at[0, alt, i - 1], back_rs.at[0, alt, i - 1], plane_peer(i))

        def out4(half, slots, i):
            return remote(book_s.at[alt, half, slots], book_s.at[alt, half, slots],
                          relay_ss.at[0, alt, i], relay_rs.at[0, alt, i], mate)

        each_peer(lambda i: out3(i, chip).start())
        if alt == ALTS - 1:
            up = jnp.concatenate(
                [total[high + 8 * i : high + 8 * i + 8] / counts[owned + i : owned + i + 1]
                 for i in range(owned)], axis=0,
            )
            lanes = lax.broadcasted_iota(jnp.int32, (8, HALF), 1)
            diagonal = lax.broadcasted_iota(jnp.int32, (8, HALF), 0) == lax.rem(lanes, 8)
            for i in range(owned):
                for q in range(K // 16):
                    half = low if q < K // 32 else up
                    picked = jnp.take_along_axis(
                        half[8 * i : 8 * i + 8], lanes // 8 + 16 * (q % 8), axis=1,
                        mode="promise_in_bounds",
                    )
                    words_ref[i : i + 1, HALF * q : HALF * q + HALF] = jnp.sum(
                        jnp.where(diagonal, picked, 0.0), axis=0, keepdims=True
                    )

        def relay(dy, first_slot):
            each(max(1, side * dy), side * dy + side,
                 lambda i: out3(i, chip_from(i)).wait_recv())
            out4(core, pl.ds(first_slot, side), dy).start()

        def settle(dy, first_slot):
            out4(other_core, pl.ds(first_slot, side), dy).wait_recv()
            rebuild(alt, first_slot)

        each_row(ROW_ORDER[:2], relay)
        each_row(ROW_ORDER[:1], settle)
        each_row(ROW_ORDER[2:3], relay)
        each_row(ROW_ORDER[1:2], settle)
        each_row(ROW_ORDER[3:], relay)
        each_row(ROW_ORDER[2:], settle)

        def gone(i):
            out1(i).wait_send()
            out3(i, chip).wait_send()

        def all_gone():
            each(1, chips, gone)
            each(1, group, lambda i: out2(i, me_g).wait_send())
            each_row(ROW_ORDER, lambda dy, at: out4(core, pl.ds(at, side), dy).wait_send())

        pending.append(all_gone)

    def rebuild(alt, first_slot):
        def step(at, carry):
            table = jnp.concatenate([book_s[alt, 0, at], book_s[alt, 1, at]], axis=0).astype(F32)
            for pair in range(owned):
                pieces = []
                for sub in range(2):
                    local = 2 * pair + sub
                    m = at * (2 * owned) + local
                    words = table[8 * local : 8 * local + 8, :]
                    column = ucol_s[pl.ds(pl.multiple_of(8 * m, 8), 8), :] / ccol_s[pl.ds(m, 1), :]
                    row_pieces = []
                    code_row = codes_s[pl.ds(m, 1), :]
                    for part in range(rows // HALF):
                        code = jnp.broadcast_to(
                            code_row[:, HALF * part : HALF * part + HALF], (8, HALF)
                        )
                        low = jnp.take_along_axis(
                            words, jnp.bitwise_and(code, HALF - 1), axis=1,
                            mode="promise_in_bounds",
                        )
                        row_pieces.append(jnp.where(code >= HALF, column, low))
                    pieces.append(jnp.concatenate(row_pieces, axis=1))
                spot = pl.multiple_of(at * 16 * owned + 16 * pair, 16)
                rec_s[pl.ds(spot, 16), :] = jnp.concatenate(pieces, axis=0).astype(BF16)
            return carry

        lax.fori_loop(first_slot, first_slot + side, step, 0)

    def reduce_cross(alt):
        gives = []
        for c, (start, size) in enumerate(CUTS):
            give_c, mate_c = pieces_c[c][0], pieces_c[c][1]
            at = pl.multiple_of(other_core * wide + start, HALF)
            give_c[alt, 0] = dot(rec_s[...], resid_s[:, pl.ds(at, size)]).astype(BF16).reshape(
                chips, tall, size
            )
            give = remote(give_c.at[alt, 0], mate_c.at[alt],
                          mate_ss.at[1 + c, alt], mate_rs.at[1 + c, alt], mate)
            give.start()
            gives.append(give)

        def out1(c, i):
            give_c, plane_c = pieces_c[c][0], pieces_c[c][2]
            return remote(give_c.at[alt, 1, chip_to(i)], plane_c.at[alt, i - 1],
                          plane_ss.at[1 + c, alt, i - 1], plane_rs.at[1 + c, alt, i - 1],
                          plane_peer(i))

        def out2(c, i, slot):
            z_c = pieces_c[c][3]
            return remote(z_c.at[alt, slot], z_c.at[alt, slot],
                          z_ss.at[1 + c, alt, i - 1], z_rs.at[1 + c, alt, i - 1], z_peer(i))

        def out3(c, i, slot):
            cross_s = pieces_c[c][4]
            return remote(cross_s.at[alt, core, slot], cross_s.at[alt, core, slot],
                          back_ss.at[1 + c, alt, i - 1], back_rs.at[1 + c, alt, i - 1],
                          plane_peer(i))

        def out4(c, half, slots, i):
            cross_s = pieces_c[c][4]
            return remote(cross_s.at[alt, half, slots], cross_s.at[alt, half, slots],
                          relay_ss.at[1 + c, alt, i], relay_rs.at[1 + c, alt, i], mate)

        for c, (start, size) in enumerate(CUTS):
            give_c, mate_c, own_c = pieces_c[c][0], pieces_c[c][1], pieces_c[c][5]
            at = pl.multiple_of(core * wide + start, HALF)
            own_c[...] = dot(rec_s[...], resid_s[:, pl.ds(at, size)]).reshape(chips, tall, size)
            gives[c].wait_recv()

            def go1(i):
                to = chip_to(i)
                give_c[alt, 1, to] = (own_c[to] + mate_c[alt, to].astype(F32)).astype(BF16)
                out1(c, i).start()

            each_peer(go1)
        flush()
        for c in range(len(CUTS)):
            mate_c, plane_c, z_c, own_c = (pieces_c[c][k] for k in (1, 2, 3, 5))

            def take1(i, acc):
                out1(c, i).wait_recv()
                return acc + plane_c[alt, i - 1].astype(F32)

            acc = own_c[chip] + mate_c[alt, chip].astype(F32)
            z_c[alt, me_g] = lax.fori_loop(1, chips, take1, acc).astype(BF16)
            each(1, group, lambda i: out2(c, i, me_g).start())
        for c in range(len(CUTS)):
            z_c, cross_s = pieces_c[c][3], pieces_c[c][4]
            each(1, group, lambda i: out2(c, i, z_from(i)).wait_recv())
            total = z_c[alt, 0].astype(F32)
            for g in range(1, group):
                total = total + z_c[alt, g].astype(F32)
            cross_s[alt, core, chip] = (total * (1.0 / total_rows)).astype(BF16)
            each_peer(lambda i: out3(c, i, chip).start())
        for c, (start, size) in enumerate(CUTS):
            cross_s = pieces_c[c][4]

            def relay(dy, first_slot):
                each(max(1, side * dy), side * dy + side,
                     lambda i: out3(c, i, chip_from(i)).wait_recv())
                out4(c, core, pl.ds(first_slot, side), dy).start()

            each_row(ROW_ORDER, relay)
            each_row(ROW_ORDER, lambda dy, at: out4(
                c, other_core, pl.ds(at, side), dy).wait_recv())
            for half in range(2):
                at = half * wide + start
                whole_s[:, at : at + size] = cross_s[alt, half].reshape(width, size)
            part = jnp.concatenate(
                [whole_s[:, half * wide + start : half * wide + start + size]
                 for half in range(2)], axis=1,
            )
            if c == 0:
                gram_s[...] = dot_nt(part, part)
            else:
                gram_s[...] += dot_nt(part, part)

        def all_gone():
            for c in range(len(CUTS)):

                def gone(i):
                    out1(c, i).wait_send()
                    out3(c, i, chip).wait_send()

                each(1, chips, gone)
                each(1, group, lambda i: out2(c, i, me_g).wait_send())
                each_row(ROW_ORDER, lambda dy, at: out4(
                    c, core, pl.ds(at, side), dy).wait_send())
                gives[c].wait_send()

        pending.append(all_gone)

    pending = []

    def flush():
        while pending:
            pending.pop(0)()

    def polar():
        blocks = [slice(at, at + width // 2) for at in range(0, width, width // 2)]
        square = jnp.zeros((8, width), F32)
        for block in blocks:
            gram = gram_s[block, :]
            square = square + jnp.sum((gram * gram).reshape(width // 16, 8, width), axis=0)
            low_s[block, :] = gram.astype(BF16)
        norm_square = jnp.sqrt(jnp.sum(square) + EPSILON)
        inv_square = 1.0 / norm_square
        inv_scale = jnp.sqrt(inv_square)
        near, far = 1.5 * inv_scale, 0.5 * inv_scale * inv_square
        for block in blocks:
            current = near * whole_s[block, :].astype(F32) - far * dot(low_s[block, :], whole_s[...])
            gram_s[block, :] = current
            rt_s[block, :] = current.astype(BF16)
        for block in blocks:
            low_s[block, :] = dot_nt(rt_s[block, :], rt_s[...]).astype(BF16)
        for block in blocks:
            whole_s[block, :] = (
                1.5 * gram_s[block, :] - 0.5 * dot(low_s[block, :], rt_s[...])
            ).astype(BF16)

    for alt in range(ALTS):
        if alt == 0:
            for load in loads[3:]:
                load.wait()
            rot_s[...] = dot(resid_s[...], gram_s[...].astype(BF16)).astype(BF16)
        else:
            rot_s[...] = dot_nt(resid_s[...], whole_s[...]).astype(BF16)
        local_sums(alt)
        if alt == 0:
            pl.semaphore_wait(barrier, chips + group - 1)
        reduce_sums(alt)
        reduce_cross(alt)
        polar()
    flush()


def per_device(vectors, centroids, list_ids, codes, rotation):
    rows, width = vectors.shape
    subspaces = codes.shape[1]
    sub_width = width // subspaces
    within = lax.axis_size("within")
    group = lax.axis_size("group")
    owned = subspaces // within
    high = owned * sub_width
    chips = within // 2
    dma = pltpu.SemaphoreType.DMA
    vmem = pl.BlockSpec(memory_space=pltpu.VMEM)
    kinds = 1 + len(CUTS)
    scratch = [
        pltpu.VMEM((centroids.shape[0], width), F32),
        pltpu.VMEM((1, rows), jnp.int32),
        pltpu.VMEM((subspaces, rows), jnp.int32),
        dma((5,)),
        pltpu.VMEM((rows, width), BF16),
        pltpu.VMEM((subspaces, HOT, rows), BF16),
        pltpu.VMEM((ALTS, 8, HALF), F32),
        pltpu.VMEM((ALTS, 8, HALF), F32),
        pltpu.VMEM((width, HALF), F32),
        pltpu.VMEM((HALF, HALF), F32),
        pltpu.VMEM((8, HALF), F32),
        pltpu.VMEM((width, rows), BF16),
        pltpu.VMEM((width, width), BF16),
        pltpu.VMEM((width, width), BF16),
        pltpu.VMEM((width, width), F32),
        pltpu.VMEM((ALTS, chips, 2, 2 * high, HALF), F32),
        pltpu.VMEM((ALTS, chips, 2 * high, HALF), F32),
        pltpu.VMEM((ALTS, chips, 2 * high, HALF), BF16),
        pltpu.VMEM((ALTS, chips - 1, 2 * high, HALF), BF16),
        pltpu.VMEM((ALTS, group, 2 * high, HALF), BF16),
        pltpu.VMEM((ALTS, 2, chips, high, HALF), BF16),
        dma((ALTS,)), dma((ALTS,)),
        dma((kinds, ALTS)), dma((kinds, ALTS)),
        dma((kinds, ALTS, chips - 1)), dma((kinds, ALTS, chips - 1)),
        dma((kinds, ALTS, group - 1)), dma((kinds, ALTS, group - 1)),
        dma((kinds, ALTS, chips - 1)), dma((kinds, ALTS, chips - 1)),
        dma((kinds, ALTS, chips)), dma((kinds, ALTS, chips)),
    ]
    for start, size in CUTS:
        block = (width // chips, size)
        scratch += [
            pltpu.VMEM((ALTS, 2, chips) + block, BF16),
            pltpu.VMEM((ALTS, chips) + block, BF16),
            pltpu.VMEM((ALTS, chips - 1) + block, BF16),
            pltpu.VMEM((ALTS, group) + block, BF16),
            pltpu.VMEM((ALTS, 2, chips) + block, BF16),
            pltpu.VMEM((chips,) + block, F32),
        ]
    resid, turned, words = pl.pallas_call(
        functools.partial(whole_kernel, within, group),
        out_shape=(
            jax.ShapeDtypeStruct((rows, width), BF16),
            jax.ShapeDtypeStruct((width, width), BF16),
            jax.ShapeDtypeStruct((owned, sub_width * K), F32),
        ),
        in_specs=[pl.BlockSpec(memory_space=pltpu.HBM)] * 5,
        out_specs=(vmem, vmem, vmem),
        scratch_shapes=scratch,
        compiler_params=pltpu.CompilerParams(
            vmem_limit_bytes=VMEM_LIMIT, collective_id=0, has_side_effects=True
        ),
    )(*[pltpu.with_memory_space_constraint(x, pltpu.HBM)
        for x in (vectors, centroids, list_ids.reshape(1, rows), codes.T, rotation)])
    return dot_nt(resid, turned).astype(BF16), words


def solution(mesh):
    in_specs = (
        P(("group", "within"), None),
        P(("group", "within"), None),
        P(("group", "within")),
        P(("group", "within"), None),
        P(),
    )
    out_specs = (P(("group", "within"), None), P("within", None))
    return jax.shard_map(
        per_device, mesh=mesh, in_specs=in_specs, out_specs=out_specs, check_vma=False
    )
```

```python
import functools

import jax
import jax.numpy as jnp
from jax import lax
from jax.experimental import pallas as pl
from jax.experimental.pallas import tpu as pltpu
from jax.sharding import PartitionSpec as P

K = 256
HALF = K // 2
HOT = HALF + 16
ALTS = 2
EPSILON = 1e-06
BATCH = 8
ROW_ORDER = (0, 1, 3, 2)
CUTS = ((0, 128), (128, 128), (256, 128))
MESH_ID = pl.DeviceIdType.MESH
NT = (((1,), (1,)), ((), ()))
VMEM_LIMIT = 48 * 1024 * 1024
F32, BF16 = jnp.float32, jnp.bfloat16


def dot_nt(left, right):
    return lax.dot_general(left, right, NT, preferred_element_type=F32)


def dot(left, right):
    return jnp.dot(left, right, preferred_element_type=F32)


def split_count(count):
    upper = jnp.floor(count * (1.0 / 256.0))
    return count - 256.0 * upper, upper


def whole_kernel(within, group, vec_ref, cen_ref, ids_ref, codes_ref, rotation_ref,
                 resid_s, whole_s, words_ref, *scratch):
    (cen_s, ids_s, codes_s, load_sem, rot_s, hot_s, urow_s, other_s, ucol_s, ccol_s, cnt_s, rec_s, rt_s, low_s, gram_s,
     table_s, mate_t, send_t, plane_t, z_t, book_s,
     pair_ss, pair_rs, mate_ss, mate_rs, plane_ss, plane_rs, z_ss, z_rs,
     back_ss, back_rs, relay_ss, relay_rs) = scratch[:33]
    pieces_c = [scratch[33 + 6 * c : 39 + 6 * c] for c in range(len(CUTS))]
    rows, width = vec_ref.shape
    lists = cen_ref.shape[0]
    subspaces = codes_s.shape[0]
    chips = within // 2
    side = 4
    total_rows = rows * within * group
    owned = subspaces // within
    high = 8 * owned
    me_g = lax.axis_index("group")
    me_w = lax.axis_index("within")
    core = lax.rem(me_w, 2)
    chip = me_w // 2
    chip_y, chip_x = chip // side, lax.rem(chip, side)
    other_core = 1 - core
    mate = (me_g, me_w + 1 - 2 * core)
    device = me_g * within + me_w
    wide = width // 2
    tall = width // chips

    def chip_to(i):
        return lax.rem(chip_y + i // side, side) * side + lax.rem(chip_x + lax.rem(i, side), side)

    def chip_from(i):
        return lax.rem(chip_y + side - i // side, side) * side + lax.rem(
            chip_x + side - lax.rem(i, side), side
        )

    def plane_peer(i):
        return (me_g, 2 * chip_to(i) + core)

    def z_from(i):
        return lax.rem(me_g + group - lax.rem(3 * i, group), group)

    def z_peer(i):
        return (lax.rem(me_g + lax.rem(3 * i, group), group), me_w)

    def remote(src, dst, ss, rs, where):
        return pltpu.make_async_remote_copy(
            src_ref=src, dst_ref=dst, send_sem=ss, recv_sem=rs,
            device_id=where, device_id_type=MESH_ID,
        )

    def each(start, stop, body):
        def step(i, carry):
            body(i)
            return carry

        lax.fori_loop(start, stop, step, 0)

    def each_peer(body):
        each(2 * side, chips, body)
        each(side, 2 * side, body)
        each(1, side, body)

    def each_row(start, body):
        for dy in start:
            body(dy, side * lax.rem(chip_y + side - dy, side))

    loads = [
        pltpu.make_async_copy(src, dst, load_sem.at[k])
        for k, (src, dst) in enumerate((
            (ids_ref, ids_s), (cen_ref, cen_s), (vec_ref, rot_s),
            (codes_ref, codes_s), (rotation_ref, gram_s),
        ))
    ]
    for load in loads:
        load.start()

    barrier = pltpu.get_barrier_semaphore()
    pl.semaphore_signal(barrier, inc=1, device_id=mate, device_id_type=MESH_ID)
    each(1, chips, lambda i: pl.semaphore_signal(
        barrier, inc=1, device_id=plane_peer(i), device_id_type=MESH_ID))
    each(1, group, lambda i: pl.semaphore_signal(
        barrier, inc=1, device_id=z_peer(i), device_id_type=MESH_ID))

    for load in loads[:3]:
        load.wait()
    local_list = jnp.broadcast_to(lax.rem(ids_s[...], lists), (lists, rows))
    pick = jnp.where(lax.broadcasted_iota(jnp.int32, (lists, rows), 0) == local_list, 1.0, 0.0)
    pick = jnp.concatenate([pick, pick, pick, jnp.zeros((lists, rows), F32)], axis=0)
    pick = pick.T.astype(BF16)
    centre = cen_s[...]
    parts = []
    for part in range(3):
        parts.append(centre.astype(BF16).astype(F32))
        centre = centre - parts[-1]
    parts = jnp.concatenate(parts + [jnp.zeros((lists, width), F32)], axis=0).astype(BF16)
    resid_s[...] = (rot_s[...].astype(F32) - dot(pick, parts)).astype(BF16)

    urow_s[...] = jnp.zeros_like(urow_s)
    lane = lax.broadcasted_iota(jnp.int32, (1, HALF), 1)
    group_row = lax.broadcasted_iota(jnp.int32, (HALF, HALF), 0)
    lane_full = lax.broadcasted_iota(jnp.int32, (HALF, HALF), 1)

    def local_sums(alt):
        first = alt == 0
        levels = lax.broadcasted_iota(jnp.int32, (HOT, rows), 0).astype(F32).astype(BF16)
        per_block = HALF // 8

        def block(b, counts):
            at = pl.multiple_of(b * HALF, HALF)
            right = rot_s[:, pl.ds(at, HALF)]
            if first:
                right = jnp.concatenate([right, jnp.ones((rows, HALF), BF16)], axis=1)
            total = jnp.zeros((HOT, HALF), F32)
            for start in range(0, per_block, BATCH):
                m0 = b * per_block + start
                if first:
                    for i in range(BATCH):
                        code = jnp.minimum(codes_s[pl.ds(m0 + i, 1), :], HALF).astype(F32).astype(BF16)
                        hot_s[m0 + i] = jnp.where(levels == code, jnp.bfloat16(1), jnp.bfloat16(0))
                hots = hot_s[pl.ds(m0, BATCH)].reshape(BATCH * HOT, rows)
                out = dot(hots, right)
                for i in range(BATCH):
                    at = 8 * (start + i)
                    here = (lane >= at) & (lane < at + 8)
                    mine = out[i * HOT : i * HOT + HOT]
                    total = jnp.where(here, mine[:, 0:HALF], total)
                    if first:
                        counts = jnp.where(lane == m0 + i, mine[:, HALF : 2 * HALF], counts)
            flipped = total[0:HALF].T
            for i in range(per_block):
                m = b * per_block + i
                w = m // owned
                spot = pl.multiple_of(8 * (m - w * owned), 8)
                table_s[alt, w // 2, lax.rem(w, 2), pl.ds(spot, 8), :] = flipped[8 * i : 8 * i + 8]
            urow_s[alt, pl.ds(b, 1), :] = total[HALF : HALF + 1]
            return counts

        counts = lax.fori_loop(0, width // HALF, block, jnp.zeros((HOT, HALF), F32))
        if first:
            urow_s[0, pl.ds(width // HALF, 1), :] = counts[HALF : HALF + 1]
            rec_c = counts[0:HALF].T
            upper = jnp.broadcast_to(urow_s[0].T[:, width // HALF : width // HALF + 1], (HALF, HALF))
            upper = jnp.where(lane_full == lax.rem(device + group_row, HALF), upper, 0.0)
            for w in range(within):
                for i in range(owned):
                    m = w * owned + i
                    table_s[0, w // 2, w % 2, high + i : high + i + 1, :] = rec_c[m : m + 1]
                    table_s[0, w // 2, w % 2, high + owned + i : high + owned + i + 1, :] = upper[
                        m : m + 1
                    ]
        else:
            columns = urow_s[alt].T
            for b in range(width // HALF):
                upper = jnp.broadcast_to(columns[:, b : b + 1], (HALF, HALF))
                spot = lax.rem(device + b * per_block + group_row // 8, HALF)
                upper = jnp.where(lane_full == spot, upper, 0.0)
                for i in range(per_block):
                    m = b * per_block + i
                    w = m // owned
                    at = high + 8 * (m % owned)
                    table_s[alt, w // 2, w % 2, at : at + 8, :] = upper[8 * i : 8 * i + 8]

    def reduce_sums(alt):
        size = high + 8 if alt == 0 else 2 * high
        sent = high + 16 if alt == 0 else 2 * high
        span = pl.ds(0, size)
        span16 = pl.ds(0, sent)

        def pack(part):
            if alt > 0:
                return part.astype(BF16)
            less, more = split_count(part[high : high + 8])
            return jnp.concatenate([part[0:high], less, more], axis=0).astype(BF16)

        def unpack(part):
            part = part.astype(F32)
            if alt > 0:
                return part
            count = part[high : high + 8] + 256.0 * part[high + 8 : high + 16]
            return jnp.concatenate([part[0:high], count], axis=0)

        give = remote(table_s.at[alt, :, other_core, span, :], mate_t.at[alt, :, span, :],
                      mate_ss.at[0, alt], mate_rs.at[0, alt], mate)
        give.start()
        swap = remote(urow_s.at[alt], other_s.at[alt], pair_ss.at[alt], pair_rs.at[alt],
                      (lax.rem(me_g + group // 2, group), me_w))
        swap.start()
        give.wait()

        def out1(i):
            return remote(send_t.at[alt, chip_to(i), span16, :],
                          plane_t.at[alt, i - 1, span16, :],
                          plane_ss.at[0, alt, i - 1], plane_rs.at[0, alt, i - 1], plane_peer(i))

        def go1(i):
            to = chip_to(i)
            send_t[alt, to, span16, :] = pack(
                table_s[alt, to, core, span, :] + mate_t[alt, to, span, :]
            )
            out1(i).start()

        each_peer(go1)
        flush()

        def take1(i, acc):
            out1(i).wait_recv()
            return acc + unpack(plane_t[alt, i - 1, span16, :])

        acc = table_s[alt, chip, core, span, :] + mate_t[alt, chip, span, :]
        z_t[alt, me_g, span16, :] = pack(lax.fori_loop(1, chips, take1, acc))

        def out2(i, slot):
            return remote(z_t.at[alt, slot, span16, :], z_t.at[alt, slot, span16, :],
                          z_ss.at[0, alt, i - 1], z_rs.at[0, alt, i - 1], z_peer(i))

        each(1, group, lambda i: out2(i, me_g).start())
        swap.wait()
        columns = (urow_s[alt] + other_s[alt]).T
        for b in range(width // HALF):
            ucol_s[b * HALF : b * HALF + HALF, :] = jnp.broadcast_to(
                columns[:, b : b + 1], (HALF, HALF)
            )
        if alt == 0:
            at = width // HALF
            ccol_s[...] = jnp.broadcast_to(columns[:, at : at + 1], (HALF, HALF)) + 1.0
        each(1, group, lambda i: out2(i, z_from(i)).wait_recv())
        total = unpack(z_t[alt, 0, span16, :])
        for g in range(1, group):
            total = total + unpack(z_t[alt, g, span16, :])
        if alt == 0:
            cnt_s[...] = total[high : high + 8] + 1.0
        counts = cnt_s[...]
        low = jnp.concatenate(
            [total[8 * i : 8 * i + 8] / counts[i : i + 1] for i in range(owned)], axis=0
        )
        book_s[alt, core, chip] = low.astype(BF16)

        def out3(i, slot):
            return remote(book_s.at[alt, core, slot], book_s.at[alt, core, slot],
                          back_ss.at[0, alt, i - 1], back_rs.at[0, alt, i - 1], plane_peer(i))

        def out4(half, slots, i):
            return remote(book_s.at[alt, half, slots], book_s.at[alt, half, slots],
                          relay_ss.at[0, alt, i], relay_rs.at[0, alt, i], mate)

        each_peer(lambda i: out3(i, chip).start())
        if alt == ALTS - 1:
            up = jnp.concatenate(
                [total[high + 8 * i : high + 8 * i + 8] / counts[owned + i : owned + i + 1]
                 for i in range(owned)], axis=0,
            )
            lanes = lax.broadcasted_iota(jnp.int32, (8, HALF), 1)
            diagonal = lax.broadcasted_iota(jnp.int32, (8, HALF), 0) == lax.rem(lanes, 8)
            for i in range(owned):
                for q in range(K // 16):
                    half = low if q < K // 32 else up
                    picked = jnp.take_along_axis(
                        half[8 * i : 8 * i + 8], lanes // 8 + 16 * (q % 8), axis=1,
                        mode="promise_in_bounds",
                    )
                    words_ref[i : i + 1, HALF * q : HALF * q + HALF] = jnp.sum(
                        jnp.where(diagonal, picked, 0.0), axis=0, keepdims=True
                    )

        def relay(dy, first_slot):
            each(max(1, side * dy), side * dy + side,
                 lambda i: out3(i, chip_from(i)).wait_recv())
            out4(core, pl.ds(first_slot, side), dy).start()

        def settle(dy, first_slot):
            out4(other_core, pl.ds(first_slot, side), dy).wait_recv()
            rebuild(alt, first_slot)

        each_row(ROW_ORDER[:2], relay)
        each_row(ROW_ORDER[:1], settle)
        each_row(ROW_ORDER[2:3], relay)
        each_row(ROW_ORDER[1:2], settle)
        each_row(ROW_ORDER[3:], relay)
        each_row(ROW_ORDER[2:], settle)

        def gone(i):
            out1(i).wait_send()
            out3(i, chip).wait_send()

        def all_gone():
            each(1, chips, gone)
            each(1, group, lambda i: out2(i, me_g).wait_send())
            each_row(ROW_ORDER, lambda dy, at: out4(core, pl.ds(at, side), dy).wait_send())

        pending.append(all_gone)

    def rebuild(alt, first_slot):
        def step(at, carry):
            table = jnp.concatenate([book_s[alt, 0, at], book_s[alt, 1, at]], axis=0).astype(F32)
            for pair in range(owned):
                pieces = []
                for sub in range(2):
                    local = 2 * pair + sub
                    m = at * (2 * owned) + local
                    words = table[8 * local : 8 * local + 8, :]
                    column = ucol_s[pl.ds(pl.multiple_of(8 * m, 8), 8), :] / ccol_s[pl.ds(m, 1), :]
                    row_pieces = []
                    code_row = codes_s[pl.ds(m, 1), :]
                    for part in range(rows // HALF):
                        code = jnp.broadcast_to(
                            code_row[:, HALF * part : HALF * part + HALF], (8, HALF)
                        )
                        low = jnp.take_along_axis(
                            words, jnp.bitwise_and(code, HALF - 1), axis=1,
                            mode="promise_in_bounds",
                        )
                        row_pieces.append(jnp.where(code >= HALF, column, low))
                    pieces.append(jnp.concatenate(row_pieces, axis=1))
                spot = pl.multiple_of(at * 16 * owned + 16 * pair, 16)
                rec_s[pl.ds(spot, 16), :] = jnp.concatenate(pieces, axis=0).astype(BF16)
            return carry

        lax.fori_loop(first_slot, first_slot + side, step, 0)

    def reduce_cross(alt):
        gives = []
        for c, (start, size) in enumerate(CUTS):
            give_c, mate_c = pieces_c[c][0], pieces_c[c][1]
            at = pl.multiple_of(other_core * wide + start, HALF)
            give_c[alt, 0] = dot(rec_s[...], resid_s[:, pl.ds(at, size)]).astype(BF16).reshape(
                chips, tall, size
            )
            give = remote(give_c.at[alt, 0], mate_c.at[alt],
                          mate_ss.at[1 + c, alt], mate_rs.at[1 + c, alt], mate)
            give.start()
            gives.append(give)

        def out1(c, i):
            give_c, plane_c = pieces_c[c][0], pieces_c[c][2]
            return remote(give_c.at[alt, 1, chip_to(i)], plane_c.at[alt, i - 1],
                          plane_ss.at[1 + c, alt, i - 1], plane_rs.at[1 + c, alt, i - 1],
                          plane_peer(i))

        def out2(c, i, slot):
            z_c = pieces_c[c][3]
            return remote(z_c.at[alt, slot], z_c.at[alt, slot],
                          z_ss.at[1 + c, alt, i - 1], z_rs.at[1 + c, alt, i - 1], z_peer(i))

        def out3(c, i, slot):
            cross_s = pieces_c[c][4]
            return remote(cross_s.at[alt, core, slot], cross_s.at[alt, core, slot],
                          back_ss.at[1 + c, alt, i - 1], back_rs.at[1 + c, alt, i - 1],
                          plane_peer(i))

        def out4(c, half, slots, i):
            cross_s = pieces_c[c][4]
            return remote(cross_s.at[alt, half, slots], cross_s.at[alt, half, slots],
                          relay_ss.at[1 + c, alt, i], relay_rs.at[1 + c, alt, i], mate)

        for c, (start, size) in enumerate(CUTS):
            give_c, mate_c, own_c = pieces_c[c][0], pieces_c[c][1], pieces_c[c][5]
            at = pl.multiple_of(core * wide + start, HALF)
            own_c[...] = dot(rec_s[...], resid_s[:, pl.ds(at, size)]).reshape(chips, tall, size)
            gives[c].wait_recv()

            def go1(i):
                to = chip_to(i)
                give_c[alt, 1, to] = (own_c[to] + mate_c[alt, to].astype(F32)).astype(BF16)
                out1(c, i).start()

            each_peer(go1)
        flush()
        for c in range(len(CUTS)):
            mate_c, plane_c, z_c, own_c = (pieces_c[c][k] for k in (1, 2, 3, 5))

            def take1(i, acc):
                out1(c, i).wait_recv()
                return acc + plane_c[alt, i - 1].astype(F32)

            acc = own_c[chip] + mate_c[alt, chip].astype(F32)
            z_c[alt, me_g] = lax.fori_loop(1, chips, take1, acc).astype(BF16)
            each(1, group, lambda i: out2(c, i, me_g).start())
        for c in range(len(CUTS)):
            z_c, cross_s = pieces_c[c][3], pieces_c[c][4]
            each(1, group, lambda i: out2(c, i, z_from(i)).wait_recv())
            total = z_c[alt, 0].astype(F32)
            for g in range(1, group):
                total = total + z_c[alt, g].astype(F32)
            cross_s[alt, core, chip] = (total * (1.0 / total_rows)).astype(BF16)
            each_peer(lambda i: out3(c, i, chip).start())
        for c, (start, size) in enumerate(CUTS):
            cross_s = pieces_c[c][4]

            def relay(dy, first_slot):
                each(max(1, side * dy), side * dy + side,
                     lambda i: out3(c, i, chip_from(i)).wait_recv())
                out4(c, core, pl.ds(first_slot, side), dy).start()

            each_row(ROW_ORDER, relay)
            each_row(ROW_ORDER, lambda dy, at: out4(
                c, other_core, pl.ds(at, side), dy).wait_recv())
            for half in range(2):
                at = half * wide + start
                whole_s[:, at : at + size] = cross_s[alt, half].reshape(width, size)
            part = jnp.concatenate(
                [whole_s[:, half * wide + start : half * wide + start + size]
                 for half in range(2)], axis=1,
            )
            if c == 0:
                gram_s[...] = dot_nt(part, part)
            else:
                gram_s[...] += dot_nt(part, part)

        def all_gone():
            for c in range(len(CUTS)):

                def gone(i):
                    out1(c, i).wait_send()
                    out3(c, i, chip).wait_send()

                each(1, chips, gone)
                each(1, group, lambda i: out2(c, i, me_g).wait_send())
                each_row(ROW_ORDER, lambda dy, at: out4(
                    c, core, pl.ds(at, side), dy).wait_send())
                gives[c].wait_send()

        pending.append(all_gone)

    pending = []

    def flush():
        while pending:
            pending.pop(0)()

    def polar():
        blocks = [slice(at, at + width // 2) for at in range(0, width, width // 2)]
        square = jnp.zeros((8, width), F32)
        for block in blocks:
            gram = gram_s[block, :]
            square = square + jnp.sum((gram * gram).reshape(width // 16, 8, width), axis=0)
            low_s[block, :] = gram.astype(BF16)
        norm_square = jnp.sqrt(jnp.sum(square) + EPSILON)
        inv_square = 1.0 / norm_square
        inv_scale = jnp.sqrt(inv_square)
        near, far = 1.5 * inv_scale, 0.5 * inv_scale * inv_square
        for block in blocks:
            current = near * whole_s[block, :].astype(F32) - far * dot(low_s[block, :], whole_s[...])
            gram_s[block, :] = current
            rt_s[block, :] = current.astype(BF16)
        for block in blocks:
            low_s[block, :] = dot_nt(rt_s[block, :], rt_s[...]).astype(BF16)
        for block in blocks:
            whole_s[block, :] = (
                1.5 * gram_s[block, :] - 0.5 * dot(low_s[block, :], rt_s[...])
            ).astype(BF16)

    for alt in range(ALTS):
        if alt == 0:
            for load in loads[3:]:
                load.wait()
            rot_s[...] = dot(resid_s[...], gram_s[...].astype(BF16)).astype(BF16)
        else:
            rot_s[...] = dot_nt(resid_s[...], whole_s[...]).astype(BF16)
        local_sums(alt)
        if alt == 0:
            pl.semaphore_wait(barrier, chips + group - 1)
        reduce_sums(alt)
        reduce_cross(alt)
        polar()
    flush()


def per_device(vectors, centroids, list_ids, codes, rotation):
    rows, width = vectors.shape
    subspaces = codes.shape[1]
    sub_width = width // subspaces
    within = lax.axis_size("within")
    group = lax.axis_size("group")
    owned = subspaces // within
    high = owned * sub_width
    chips = within // 2
    dma = pltpu.SemaphoreType.DMA
    vmem = pl.BlockSpec(memory_space=pltpu.VMEM)
    kinds = 1 + len(CUTS)
    scratch = [
        pltpu.VMEM((centroids.shape[0], width), F32),
        pltpu.VMEM((1, rows), jnp.int32),
        pltpu.VMEM((subspaces, rows), jnp.int32),
        dma((5,)),
        pltpu.VMEM((rows, width), BF16),
        pltpu.VMEM((subspaces, HOT, rows), BF16),
        pltpu.VMEM((ALTS, 8, HALF), F32),
        pltpu.VMEM((ALTS, 8, HALF), F32),
        pltpu.VMEM((width, HALF), F32),
        pltpu.VMEM((HALF, HALF), F32),
        pltpu.VMEM((8, HALF), F32),
        pltpu.VMEM((width, rows), BF16),
        pltpu.VMEM((width, width), BF16),
        pltpu.VMEM((width, width), BF16),
        pltpu.VMEM((width, width), F32),
        pltpu.VMEM((ALTS, chips, 2, 2 * high, HALF), F32),
        pltpu.VMEM((ALTS, chips, 2 * high, HALF), F32),
        pltpu.VMEM((ALTS, chips, 2 * high, HALF), BF16),
        pltpu.VMEM((ALTS, chips - 1, 2 * high, HALF), BF16),
        pltpu.VMEM((ALTS, group, 2 * high, HALF), BF16),
        pltpu.VMEM((ALTS, 2, chips, high, HALF), BF16),
        dma((ALTS,)), dma((ALTS,)),
        dma((kinds, ALTS)), dma((kinds, ALTS)),
        dma((kinds, ALTS, chips - 1)), dma((kinds, ALTS, chips - 1)),
        dma((kinds, ALTS, group - 1)), dma((kinds, ALTS, group - 1)),
        dma((kinds, ALTS, chips - 1)), dma((kinds, ALTS, chips - 1)),
        dma((kinds, ALTS, chips)), dma((kinds, ALTS, chips)),
    ]
    for start, size in CUTS:
        block = (width // chips, size)
        scratch += [
            pltpu.VMEM((ALTS, 2, chips) + block, BF16),
            pltpu.VMEM((ALTS, chips) + block, BF16),
            pltpu.VMEM((ALTS, chips - 1) + block, BF16),
            pltpu.VMEM((ALTS, group) + block, BF16),
            pltpu.VMEM((ALTS, 2, chips) + block, BF16),
            pltpu.VMEM((chips,) + block, F32),
        ]
    resid, turned, words = pl.pallas_call(
        functools.partial(whole_kernel, within, group),
        out_shape=(
            jax.ShapeDtypeStruct((rows, width), BF16),
            jax.ShapeDtypeStruct((width, width), BF16),
            jax.ShapeDtypeStruct((owned, sub_width * K), F32),
        ),
        in_specs=[pl.BlockSpec(memory_space=pltpu.HBM)] * 5,
        out_specs=(vmem, vmem, vmem),
        scratch_shapes=scratch,
        compiler_params=pltpu.CompilerParams(
            vmem_limit_bytes=VMEM_LIMIT, collective_id=0, has_side_effects=True
        ),
    )(*[pltpu.with_memory_space_constraint(x, pltpu.HBM)
        for x in (vectors, centroids, list_ids.reshape(1, rows), codes.T, rotation)])
    return dot_nt(resid, turned).astype(BF16), words


def solution(mesh):
    in_specs = (
        P(("group", "within"), None),
        P(("group", "within"), None),
        P(("group", "within")),
        P(("group", "within"), None),
        P(),
    )
    out_specs = (P(("group", "within"), None), P("within", None))
    return jax.shard_map(
        per_device, mesh=mesh, in_specs=in_specs, out_specs=out_specs, check_vma=False
    )
```
